256 devices in a mesh: grp: 16 (over z, core), blk: 16 (over x, y).
Axes of the slice: x: 4, y: 4, z: 8, core: 2. Of those that a mesh axis runs over, the one named last changes fastest.
Arguments:
- patches: float32 [2048, 32, 1024], P(('grp', 'blk')), may hold values from -6 to 6
- counts: int32 [256], P(('grp', 'blk')), may hold values from 1 to 8
- moves: int32 [256, 4], P(('grp', 'blk')), may hold values from 0 to 3, as said below
- tags: int32 [16, 128], P('grp'), may hold values from 0 to 3
Outputs:
- fine: bfloat16 [2048, 64, 4096], P(('grp', 'blk'))
The draws below stay inside these ranges and needn't reach their ends.
Inputs may be any that keep to these rules, and one draw needn't show every extreme that they name: `moves`: each device holds between 1 and 8 live patches before and after every diffusion step, and hands on fewer patches than it holds at that step; in every draw some device hands on exactly 3 patches in some step.
All inputs are finite; a program needn't handle non-finite values.
Results may differ from the reference program's by a relative error of at most 0.001.
Values sent between devices are 32-bit elements; how exact they have to be, the bound alone decides.
A program may use at most 128 MiB of HBM per device.

```python
import jax
import jax.numpy as jnp
from jax import lax

E = 32
CAP = 8
MOST = 3
STEPS = 4
NDEV = 256
NBOX = 128
NPATCH = 2048
N_GRP = 16
N_BLK = 16


def plan_loads(key):
    key = jax.random.fold_in(key, 7)
    first, second, third, fourth = jax.random.split(key, 4)
    groups = NDEV // N_BLK
    heavy = jax.random.randint(first, (groups, N_BLK), 0, 2) == 0
    large = jax.random.randint(second, (groups, N_BLK), CAP // 2, CAP + 1)
    small = jax.random.randint(third, (groups, N_BLK), 2, min(5, CAP + 1))
    live = jnp.where(heavy, large, small)
    live = live.at[:, 0].set(jnp.maximum(live[:, 0], MOST + 1))
    live = live.at[:, 1].set(jnp.minimum(live[:, 1], CAP - MOST))
    wishes = jax.random.randint(fourth, (groups, N_BLK, STEPS), 0, MOST + 1)
    wishes = wishes.at[:, 0, 0].set(MOST)
    initial = live
    columns = []
    for step in range(STEPS):
        following = jnp.roll(live, -1, axis=1)
        handed = jnp.minimum(jnp.minimum(wishes[:, :, step], live - 1), CAP - following)
        columns.append(handed)
        live = live - handed + jnp.roll(handed, 1, axis=1)
    return (initial.reshape(NDEV).astype(jnp.int32), jnp.stack(columns, -1).reshape(NDEV, STEPS).astype(jnp.int32))


def draw_counts(key, part):
    return plan_loads(key)[0]


def draw_moves(key, part):
    return plan_loads(key)[1]


def touch_ends(values, key, smallest, top_value):
    longest = values.shape.index(max(values.shape))
    spots = []
    for shift in (0, 1):
        where = [jax.random.randint(jax.random.fold_in(key, axis), (), 0, length) for axis, length in enumerate(values.shape)]
        where[longest] = (where[longest] + shift) % values.shape[longest]
        spots.append(tuple(where))
    return values.at[spots[0]].set(smallest).at[spots[1]].set(top_value)


def block_scale(rng, extent, cuts, least, high):
    factor_of = 1.0
    for dim, shards_of in cuts:
        draws = jax.random.uniform(jax.random.fold_in(jax.random.fold_in(rng, 6), dim), (shards_of,), jnp.float32, least / len(cuts), high / len(cuts))
        factor_of = factor_of * jnp.repeat(jnp.exp(draws), extent[dim] // shards_of).reshape((-1,) + (1,) * (len(extent) - 1 - dim))
    return factor_of


def gaussian(key, shape, scale, reach, cuts=(), kind=jnp.bfloat16):
    drawn = jax.random.normal(key, shape, jnp.float32) * scale
    if len(cuts) > 0:
        drawn = block_scale(key, shape, cuts, -0.22, 0.18) * drawn
    return jnp.clip(drawn, min=-reach, max=reach).astype(kind)


def setup_inputs(seed: int = 0) -> dict:
    keys = jax.random.split(jax.random.key(seed), 5)
    patches = gaussian(keys[0], (NPATCH, E, E * E), 1.0, 6.0, ((0, 256),), jnp.float32)
    counts = draw_counts(jax.random.fold_in(keys[4], 71), 0)
    moves = draw_moves(jax.random.fold_in(keys[4], 71), 0)
    tags = touch_ends(jax.random.randint(keys[3], (N_GRP, NBOX), 0, 4), jax.random.fold_in(keys[3], 1), 0, 3).astype(jnp.int32)
    return dict(patches=patches, counts=counts, moves=moves, tags=tags)


def refine_table(edge, margin):
    finer = jnp.arange(2 * edge)[:, None]
    coarse = jnp.arange(edge + 2 * margin)[None, :]
    home = finer // 2 + margin
    side = home + 2 * (finer % 2) - 1
    return (0.75 * (coarse == home) + 0.25 * (coarse == side)).astype(jnp.float32)


def refine(extended, edge):
    number = extended.shape[0]
    cube = extended.reshape(number, edge + 2, edge, edge)
    across = refine_table(edge, 1)
    inner = refine_table(edge, 0)
    highest = lax.Precision.HIGHEST
    first = jnp.einsum('fx,pxyz->pfyz', across, cube, precision=highest)
    second = jnp.einsum('gy,pfyz->pfgz', inner, first, precision=highest)
    third = jnp.einsum('hz,pfgz->pfgh', inner, second, precision=highest)
    return third.reshape(number, 2 * edge, 4 * edge * edge)


def tag_factors(tag_row, offset, capacity):
    position = offset + jnp.arange(capacity).astype(jnp.int32)
    boxes = jnp.arange(tag_row.shape[0]).astype(jnp.int32)
    picked = jnp.sum(jnp.where(position[:, None] == boxes[None, :], tag_row[None, :], 0), axis=1)
    return 1.0 + 0.5 * picked.astype(jnp.float32)


def finish(work, live, lower, upper, factors):
    capacity, edge = work.shape[0], work.shape[1]
    slots = jnp.arange(capacity).astype(jnp.int32)
    below = jnp.concatenate([lower[None], work[:-1, edge - 1]], 0)
    above = jnp.concatenate([work[1:, 0], upper[None]], 0)
    above = jnp.where((slots == live - 1)[:, None], upper[None], above)
    extended = jnp.concatenate([below[:, None], work, above[:, None]], 1)
    refined = refine(extended, edge)
    scaled = refined * factors[:, None, None]
    return jnp.where((slots < live)[:, None, None], scaled, 0.0).astype(jnp.bfloat16)


def reference(patches, counts, moves, tags):
    groups = N_GRP
    cycle = N_BLK
    field = patches.reshape(groups, cycle, CAP, E, E * E)
    field = jnp.concatenate([field, jnp.zeros((groups, cycle, MOST, E, E * E), field.dtype)], 2)
    live = counts.reshape(groups, cycle)
    handed = moves.reshape(groups, cycle, STEPS)
    cutter = jax.vmap(jax.vmap(lambda block, first: lax.dynamic_slice_in_dim(block, first, MOST, 0)))
    paster = jax.vmap(jax.vmap(lambda block, piece, first: lax.dynamic_update_slice_in_dim(block, piece, first, 0)))
    for step in range(STEPS):
        sent = handed[:, :, step]
        start = live - sent
        parcel = cutter(field, start)
        arrived = jnp.roll(parcel, 1, axis=1)
        field = paster(field, arrived, start)
        live = start + jnp.roll(sent, 1, axis=1)
    offsets = (jnp.cumsum(live, axis=1) - live).reshape(NDEV)
    work = field[:, :, :CAP].reshape(NDEV, CAP, E, E * E)
    live = live.reshape(NDEV)
    tops = work[jnp.arange(NDEV), live - 1, E - 1]
    zero_plane = jnp.zeros((1, E * E), work.dtype)
    lower = jnp.concatenate([zero_plane, tops[:-1]], 0)
    upper = jnp.concatenate([work[1:, 0, 0], zero_plane], 0)
    group_tags = jnp.repeat(tags, cycle, axis=0)

    def one_device(items):
        block, count, below, above, offset, tag_row = items
        return finish(block, count, below, above, tag_factors(tag_row, offset, CAP))

    result = lax.map(one_device, (work, live, lower, upper, offsets, group_tags))
    return result.reshape(NDEV * CAP, 2 * E, 4 * E * E)
```

```python
import jax
import jax.numpy as jnp
import numpy as np
from jax import lax
from jax.experimental import pallas as pl
from jax.experimental.pallas import tpu as pltpu
from jax.sharding import PartitionSpec as P

MOST = 3
STEPS = 4


def passed_along(block, axis, distance):
    devices = range(lax.axis_size(axis))
    route = [((i - distance) % len(devices), i) for i in devices]
    return lax.ppermute(block, axis, route)


def from_everyone(x, axis):
    devices = lax.axis_size(axis)
    return lax.all_to_all(jnp.broadcast_to(x[None], (devices, *x.shape)), axis, 0, 0, tiled=True)


def combined_pairwise(pieces, combine):
    while len(jax.tree.leaves(pieces)[0]) > 1:
        pieces = jax.vmap(combine)(*(pieces[side::2] for side in (0, 1)))
    return pieces[0]


def carried_in(x, axis, combine, identity):
    devices, place = (lax.axis_size(axis), lax.axis_index(axis))
    passed = jnp.arange(devices) < place

    def kept(part, zero, own):
        part = jnp.where(
            passed.reshape(-1, *(1 for _ in own.shape)), part, jnp.asarray(zero, own.dtype)
        )
        return part

    pieces = from_everyone(x, axis)
    return combined_pairwise(kept(pieces, identity, x), combine)


def from_behind(x, axis, by):
    devices = lax.axis_size(axis)
    pairs = [(i, i + by) for i in range(devices) if 0 <= i + by < devices]
    return lax.ppermute(x, axis, pairs)


def refine_weights():
    fine = np.arange(64)
    home, side = fine // 2, fine // 2 + 2 * (fine % 2) - 1
    grid = np.arange(32)[:, None]
    z = 0.75 * (grid == home) + 0.25 * (grid == side)
    y = np.zeros((4, 2, 2), np.float32)
    for c in range(2):
        y[c + 1, c, :] = 0.75
        y[c, c, 0] = 0.25
        y[c + 2, c, 1] = 0.25
    half = np.kron(y.reshape(4, 4), z)
    return np.concatenate([half, half], 0)

def refine_kernel(info, tags, field, lower, upper, weights, fine, rows, stage, done, in_sem, out_sem):
    slots, edge = field.shape[0], field.shape[1]
    loads = [pltpu.make_async_copy(field.at[j], rows.at[pl.ds(8 + edge * j, edge)], in_sem.at[j]) for j in range(slots)]
    for load in loads:
        load.start()
    live, offset = info[0], info[1]
    for load in loads:
        load.wait()
    rows[pl.ds(7, 1), :] = jnp.where(info[2] == 0, 0.0, lower[...])
    rows[pl.ds(8 + edge * live, 1), :] = jnp.where(info[3] == 0, 0.0, upper[...])
    lanes = lax.broadcasted_iota(jnp.int32, (2 * edge, 128), 1)
    zeros = jnp.zeros((2 * edge, 128), jnp.float32)

    def one(j, carry):
        start = pl.multiple_of(edge * j, 8)
        tag = tags[0, jnp.minimum(offset + j, tags.shape[1] - 1)]
        factor = jnp.where(j < live, 1.0 + 0.5 * tag.astype(jnp.float32), 0.0)
        for m in range(8):
            part = rows[pl.ds(start, edge + 16), pl.ds(128 * m, 128)] * factor
            home = 0.75 * part[8:8 + edge]
            quarter = 0.25 * part
            stage[m, pl.ds(0, edge, stride=2), :] = home + quarter[7:7 + edge]
            stage[m, pl.ds(1, edge, stride=2), :] = home + quarter[9:9 + edge]
        def emit(window, value):
            high = value.astype(jnp.bfloat16)
            low = (value - high.astype(jnp.float32)).astype(jnp.bfloat16)
            both = jnp.concatenate([high, low], axis=1)
            got = jnp.dot(both, weights[...], preferred_element_type=jnp.float32)
            done[j, :, pl.ds(256 * window, 256)] = got.astype(jnp.bfloat16)
        right_before = zeros
        tile = stage[0]
        left = pltpu.roll(tile, 96, 1)
        for m in range(8):
            right = pltpu.roll(tile, 32, 1)
            emit(2 * m, jnp.where(lanes < 32, right_before, right))
            right_before = right
            if m < 7:
                tile = stage[m + 1]
                left_next = pltpu.roll(tile, 96, 1)
            else:
                left_next = zeros
            emit(2 * m + 1, jnp.where(lanes < 96, left, left_next))
            left = left_next
        pltpu.make_async_copy(done.at[j], fine.at[j], out_sem.at[j]).start()
        return carry

    lax.fori_loop(0, slots, one, 0)
    for j in range(slots):
        pltpu.make_async_copy(done.at[j], fine.at[j], out_sem.at[j]).wait()

def refine(info, tags, field, lower, upper, weights):
    return pl.pallas_call(
        refine_kernel,
        out_shape=jax.ShapeDtypeStruct((8, 64, 4096), jnp.bfloat16),
        in_specs=[pl.BlockSpec(memory_space=pltpu.SMEM)] * 2 + [pl.BlockSpec(memory_space=pl.ANY)] + [pl.BlockSpec(memory_space=pltpu.VMEM)] * 3,
        out_specs=pl.BlockSpec(memory_space=pl.ANY),
        scratch_shapes=[pltpu.VMEM((272, 1024), jnp.float32), pltpu.VMEM((8, 64, 128), jnp.float32),
                        pltpu.VMEM((8, 64, 4096), jnp.bfloat16),
                        pltpu.SemaphoreType.DMA((8,)), pltpu.SemaphoreType.DMA((8,))],
        name="refine",
    )(info, tags, field, lower, upper, weights)


def add_counts(earlier, later):
    return earlier + later


def body(patches, counts, moves, tags):
    capacity, edge = (patches.shape[0], patches.shape[1])
    live = counts[0]
    padding = jnp.zeros((MOST,) + patches.shape[1:], patches.dtype)
    field = jnp.concatenate([patches, padding], 0)
    earlier = passed_along(moves, "blk", 1)
    for step in range(STEPS):
        start = live - moves[0, step]
        parcel = lax.dynamic_slice_in_dim(field, start, MOST, 0)
        arrived = passed_along(parcel, "blk", 1)
        field = lax.dynamic_update_slice_in_dim(field, arrived, start, 0)
        live = start + earlier[0, step]
    work = field[:capacity]
    offset = carried_in(live.reshape(1), "blk", add_counts, jnp.zeros((1,), jnp.int32))[0]
    top_patch = lax.dynamic_index_in_dim(work, live - 1, 0, keepdims=False)
    lower = from_behind(top_patch[edge - 1], ("grp", "blk"), 1)
    upper = from_behind(work[0, 0], ("grp", "blk"), -1)
    place = lax.axis_index("grp") * lax.axis_size("blk") + lax.axis_index("blk")
    last = lax.axis_size("grp") * lax.axis_size("blk") - 1
    info = jnp.stack([live, offset, (place > 0).astype(jnp.int32), (place < last).astype(jnp.int32)])
    weights = jnp.asarray(refine_weights(), jnp.bfloat16)
    return refine(info, tags, work, lower[None], upper[None], weights)


def solution(mesh):
    in_specs = (
        P(("grp", "blk"), None, None),
        P(("grp", "blk")),
        P(("grp", "blk"), None),
        P("grp", None),
    )
    out_specs = P(("grp", "blk"), None, None)
    return jax.shard_map(body, mesh=mesh, in_specs=in_specs, out_specs=out_specs, check_vma=False)
```

```python
import jax
import jax.numpy as jnp
import numpy as np
from jax import lax
from jax.experimental import pallas as pl
from jax.experimental.pallas import tpu as pltpu
from jax.sharding import PartitionSpec as P

MOST = 3
STEPS = 4
MESH = pl.DeviceIdType.MESH
SIDE = 4
CAP = 8
HELD = CAP - 1
OWN = SIDE * HELD
CROSS = MOST * STEPS
PARTS = 4
FAR = 1000

def exchange_kernel(counts, moves, patches, moved, planes, info, *scratch):
    scratch = list(scratch)
    def take(number):
        out = scratch[:number]
        del scratch[:number]
        return out
    pool, crossing_in, crossing_out, final = take(PARTS), take(PARTS), take(PARTS), take(PARTS)
    table, numbers, cuts, above, wanted, corner, edges, bases, tops = take(9)
    (pool_send, pool_recv, pool_local, cross_send, cross_recv, final_send, final_recv, final_local,
     meta_send, meta_recv, small, plane_send, plane_recv, base_send, base_recv, top_send) = scratch

    grp, blk = lax.axis_index("grp"), lax.axis_index("blk")
    groups, devices = lax.axis_size("grp"), lax.axis_size("blk")
    row, place = lax.div(blk, SIDE), lax.rem(blk, SIDE)
    rows_of_devices = devices // SIDE
    width = patches.shape[2] // PARTS
    depth = patches.shape[1] // SIDE
    line = grp * devices + blk
    after = lax.rem(line + 1, groups * devices)
    before = lax.rem(line + groups * devices - 1, groups * devices)
    after, before = [(lax.div(other, devices), lax.rem(other, devices)) for other in (after, before)]

    def across(k):
        return lax.rem(place + k, SIDE)

    def beside(k):
        return (grp, row * SIDE + across(k))

    def over(k):
        return (grp, lax.rem(row + k, rows_of_devices) * SIDE + place)

    def remote(src, dst, send, recv, device):
        return pltpu.make_async_remote_copy(src_ref=src, dst_ref=dst, send_sem=send, recv_sem=recv, device_id=device, device_id_type=MESH)

    def lanes(part):
        return pl.ds(width * part, width)

    def strip(home):
        return pl.ds(pl.multiple_of(home * depth, depth), depth)

    local = [pltpu.make_async_copy(patches.at[pl.ds(1, HELD), strip(place), lanes(i)], pool[i].at[pl.ds(HELD * place, HELD)], pool_local.at[i]) for i in range(PARTS)]
    ends = [pltpu.make_async_copy(patches.at[0, pl.ds(0, 8)], corner.at[0], small.at[0]),
            pltpu.make_async_copy(patches.at[0, pl.ds(patches.shape[1] - 8, 8)], corner.at[1], small.at[1])]
    for copy in ends + local:
        copy.start()
    lane = lax.broadcasted_iota(jnp.int32, (1, 128), 1)
    mine = jnp.where(lane == 0, counts[0], 0)
    for s in range(STEPS):
        mine = jnp.where(lane == 1 + s, moves[0, s], mine)
    table[blk] = mine

    barrier = pltpu.get_barrier_semaphore()
    for k in range(1, SIDE):
        pl.semaphore_signal(barrier, inc=1, device_id=beside(k), device_id_type=MESH)
    for k in range(1, rows_of_devices):
        pl.semaphore_signal(barrier, inc=1, device_id=over(k), device_id_type=MESH)
    first, last = place == 0, place == SIDE - 1
    @pl.when(last)
    def _():
        pl.semaphore_signal(barrier, inc=1, device_id=after, device_id_type=MESH)
    @pl.when(first)
    def _():
        pl.semaphore_signal(barrier, inc=1, device_id=before, device_id_type=MESH)
    pl.semaphore_wait(barrier, SIDE - 1 + rows_of_devices - 1 + jnp.where(first, 1, 0) + jnp.where(last, 1, 0))

    row_meta = [remote(table.at[blk], table.at[blk], meta_send.at[k - 1], meta_recv.at[k - 1], beside(k)) for k in range(1, SIDE)]
    for copy in row_meta:
        copy.start()
    gathers = [[remote(patches.at[pl.ds(1, HELD), strip(across(k)), lanes(i)], pool[i].at[pl.ds(HELD * place, HELD)],
                       pool_send.at[i, k - 1], pool_recv.at[i, k - 1], beside(k)) for k in range(1, SIDE)] for i in range(PARTS)]
    for part in gathers:
        for copy in part:
            copy.start()

    for copy in ends:
        copy.wait()
    edges[0] = corner[0, pl.ds(0, 1), :]
    edges[1] = corner[1, pl.ds(7, 1), :]

    for copy in row_meta:
        copy.wait_recv()
    own_row = pl.ds(row * SIDE, SIDE)
    column_meta = [remote(table.at[own_row], table.at[own_row], meta_send.at[SIDE - 2 + k], meta_recv.at[SIDE - 2 + k], over(k)) for k in range(1, rows_of_devices)]
    for copy in column_meta:
        copy.start()
    upper = remote(edges.at[0], planes.at[1], plane_send, plane_recv.at[1], before)
    upper.start()
    base = remote(edges.at[1], bases.at[place], base_send, base_recv.at[place], (grp, row * SIDE + SIDE - 1))
    base_here = pltpu.make_async_copy(edges.at[1], bases.at[SIDE - 1], base_send)
    @pl.when(jnp.logical_not(last))
    def _():
        base.start()
    @pl.when(last)
    def _():
        base_here.start()
    for copy in column_meta:
        copy.wait_recv()
    read = pltpu.make_async_copy(table, numbers, small.at[2])
    read.start()
    read.wait()

    def number(rank, column):
        return numbers[lax.rem(row * SIDE + rank - 1 + devices, devices), 0, column]

    live = [number(rank, 0) for rank in range(SIDE + 1)]
    for s in range(STEPS):
        sent = [number(rank, 1 + s) for rank in range(SIDE + 1)]
        cut = [have - gone for have, gone in zip(live, sent)]
        for rank in range(SIDE + 1):
            cuts[8 * s + rank] = cut[rank] if rank else FAR
            above[8 * s + rank] = cut[rank - 1] if rank > 1 else OWN + MOST * s
        live = [cut[0]] + [cut[rank] + sent[rank - 1] for rank in range(1, SIDE + 1)]

    def traced(rank, slot, steps):
        for s in reversed(range(steps)):
            beyond = slot - cuts[8 * s + rank]
            came = beyond >= 0
            slot = jnp.where(came, above[8 * s + rank] + beyond, slot)
            rank = jnp.where(came, rank - 1, rank)
            rank = jnp.maximum(rank, 0)
        return jnp.where(rank == 0, slot, HELD * (rank - 1) + slot - 1)

    for s in range(STEPS):
        for t in range(MOST):
            slot = cuts[8 * s + SIDE] + t
            wanted[32 + MOST * s + t] = jnp.clip(traced(jnp.int32(SIDE), slot, s), 0, OWN - 1)

    crosses = [remote(crossing_out[i], crossing_in[i], cross_send.at[i], cross_recv.at[i], over(1)) for i in range(PARTS)]

    def cross(i):
        local[i].wait()
        for copy in gathers[i]:
            copy.wait_recv()
        for n in range(CROSS):
            crossing_out[i][n] = pool[i][wanted[32 + n]]
        crosses[i].start()

    cross(0)

    def plan(n, carry):
        rank, slot = lax.div(n, HELD) + 1, lax.rem(n, HELD) + 1
        wanted[n] = jnp.clip(traced(rank, slot, STEPS), 0, OWN + CROSS - 1)
        return carry
    lax.fori_loop(0, OWN, plan, 0)

    def moved_by(rank):
        total = numbers[rank, 0, 1]
        for s in range(1, STEPS):
            total = total + numbers[rank, 0, 1 + s]
        return total

    gone_before = moved_by(lax.rem(blk + devices - 1, devices))
    info[0] = numbers[blk, 0, 0] - moved_by(blk) + gone_before
    lower_counts = jnp.int32(0)
    for rank in range(devices):
        lower_counts = lower_counts + jnp.where(rank < blk, numbers[rank, 0, 0], 0)
    info[1] = jnp.where(blk == 0, 0, lower_counts - gone_before + moved_by(devices - 1))
    info[2] = jnp.where(line > 0, 1, 0)
    info[3] = jnp.where(line < groups * devices - 1, 1, 0)

    for i in range(1, PARTS):
        cross(i)

    scatters = [[remote(final[i].at[pl.ds(HELD * across(k), HELD)], moved.at[:, strip(place), lanes(i)],
                        final_send.at[i, k - 1], final_recv.at[i, k - 1], beside(k)) for k in range(1, SIDE)] for i in range(PARTS)]
    stays = [pltpu.make_async_copy(final[i].at[pl.ds(HELD * place, HELD)], moved.at[:, strip(place), lanes(i)], final_local.at[i]) for i in range(PARTS)]
    @pl.when(last)
    def _():
        for k in range(SIDE - 1):
            remote(edges.at[1], bases.at[k], base_send, base_recv.at[k], beside(1)).wait_recv()
        base_here.wait()
    for i in range(PARTS):
        crosses[i].wait_recv()
        def pick(n, carry, i=i):
            source = wanted[n]
            own = pool[i][jnp.minimum(source, OWN - 1)]
            other = crossing_in[i][jnp.maximum(source - OWN, 0)]
            final[i][n] = jnp.where(source < OWN, own, other)
            return carry
        lax.fori_loop(0, OWN, pick, 0, unroll=7)
        for copy in scatters[i]:
            copy.start()
        stays[i].start()
        @pl.when(last)
        def _():
            for k in range(SIDE):
                top = final[i][HELD * k + jnp.maximum(live[k + 1] - 2, 0), pl.ds(depth - 1, 1), :]
                tops[k, :, lanes(i)] = jnp.where(live[k + 1] > 1, top, bases[k, :, lanes(i)])
    top_copies = [remote(tops.at[k], planes.at[0], top_send.at[k], plane_recv.at[0], beside(k + 2)) for k in range(SIDE - 2)]
    top_copies.append(remote(tops.at[SIDE - 1], planes.at[0], top_send.at[SIDE - 1], plane_recv.at[0], after))
    top_here = pltpu.make_async_copy(tops.at[SIDE - 2], planes.at[0], plane_recv.at[0])
    @pl.when(last)
    def _():
        for copy in top_copies:
            copy.start()
        top_here.start()
        for copy in top_copies:
            copy.wait_send()
    @pl.when(jnp.logical_not(last))
    def _():
        base.wait_send()
    top_copies[0].wait_recv()
    upper.wait()
    for copy in row_meta + column_meta:
        copy.wait_send()
    for i in range(PARTS):
        crosses[i].wait_send()
        for copy in gathers[i]:
            copy.wait_send()
        stays[i].wait()
        for copy in scatters[i]:
            copy.wait()

def exchange(counts, moves, patches):
    slots, edge, width = patches.shape
    part = width // PARTS
    strip = edge // SIDE
    def blocks(number):
        return [pltpu.VMEM((number, strip, part), jnp.float32)] * PARTS
    dma = pltpu.SemaphoreType.DMA
    others = SIDE - 1
    return pl.pallas_call(
        exchange_kernel,
        out_shape=(jax.ShapeDtypeStruct((HELD, edge, width), jnp.float32),
                   jax.ShapeDtypeStruct((2, 1, width), jnp.float32),
                   jax.ShapeDtypeStruct((8,), jnp.int32)),
        in_specs=[pl.BlockSpec(memory_space=pltpu.SMEM)] * 2 + [pl.BlockSpec(memory_space=pl.ANY)],
        out_specs=(pl.BlockSpec(memory_space=pl.ANY), pl.BlockSpec(memory_space=pl.ANY), pl.BlockSpec(memory_space=pltpu.SMEM)),
        scratch_shapes=blocks(OWN) + blocks(CROSS) + blocks(CROSS) + blocks(OWN) + [
            pltpu.VMEM((16, 1, 128), jnp.int32), pltpu.SMEM((16, 1, 128), jnp.int32),
            pltpu.SMEM((8 * STEPS,), jnp.int32), pltpu.SMEM((8 * STEPS,), jnp.int32), pltpu.SMEM((48,), jnp.int32),
            pltpu.VMEM((2, 8, width), jnp.float32), pltpu.VMEM((2, 1, width), jnp.float32),
            pltpu.VMEM((SIDE, 1, width), jnp.float32), pltpu.VMEM((SIDE, 1, width), jnp.float32),
            dma((PARTS, others)), dma((PARTS, others)), dma((PARTS,)), dma((PARTS,)), dma((PARTS,)),
            dma((PARTS, others)), dma((PARTS, others)), dma((PARTS,)),
            dma((2 * others,)), dma((2 * others,)), dma((3,)), dma(()), dma((2,)), dma(()), dma((SIDE,)), dma((SIDE,)),
        ],
        compiler_params=pltpu.CompilerParams(collective_id=0, has_side_effects=True),
        name="exchange",
    )(counts, moves, patches)


def refine_weights():
    fine = np.arange(64)
    home, side = fine // 2, fine // 2 + 2 * (fine % 2) - 1
    grid = np.arange(32)[:, None]
    z = 0.75 * (grid == home) + 0.25 * (grid == side)
    y = np.zeros((4, 2, 2), np.float32)
    for c in range(2):
        y[c + 1, c, :] = 0.75
        y[c, c, 0] = 0.25
        y[c + 2, c, 1] = 0.25
    half = np.kron(y.reshape(4, 4), z)
    return np.concatenate([half, half], 0)

def refine_kernel(info, tags, patches, moved, planes, weights, fine, rows, stage, done, in_sem, out_sem):
    slots, edge = patches.shape[0], patches.shape[1]
    loads = [pltpu.make_async_copy(moved.at[j - 1] if j else patches.at[0], rows.at[pl.ds(8 + edge * j, edge)], in_sem.at[j]) for j in range(slots)]
    for load in loads:
        load.start()
    live, offset = info[0], info[1]
    for load in loads:
        load.wait()
    rows[pl.ds(7, 1), :] = jnp.where(info[2] == 0, 0.0, planes[0])
    rows[pl.ds(8 + edge * live, 1), :] = jnp.where(info[3] == 0, 0.0, planes[1])
    lanes = lax.broadcasted_iota(jnp.int32, (2 * edge, 128), 1)
    zeros = jnp.zeros((2 * edge, 128), jnp.float32)

    def one(j, carry):
        start = pl.multiple_of(edge * j, 8)
        tag = tags[0, jnp.minimum(offset + j, tags.shape[1] - 1)]
        factor = jnp.where(j < live, 1.0 + 0.5 * tag.astype(jnp.float32), 0.0)
        for m in range(8):
            part = rows[pl.ds(start, edge + 16), pl.ds(128 * m, 128)] * factor
            home = 0.75 * part[8:8 + edge]
            quarter = 0.25 * part
            stage[m, pl.ds(0, edge, stride=2), :] = home + quarter[7:7 + edge]
            stage[m, pl.ds(1, edge, stride=2), :] = home + quarter[9:9 + edge]
        def emit(window, value):
            high = value.astype(jnp.bfloat16)
            low = (value - high.astype(jnp.float32)).astype(jnp.bfloat16)
            both = jnp.concatenate([high, low], axis=1)
            got = jnp.dot(both, weights[...], preferred_element_type=jnp.float32)
            done[j, :, pl.ds(256 * window, 256)] = got.astype(jnp.bfloat16)
        right_before = zeros
        tile = stage[0]
        left = pltpu.roll(tile, 96, 1)
        for m in range(8):
            right = pltpu.roll(tile, 32, 1)
            emit(2 * m, jnp.where(lanes < 32, right_before, right))
            right_before = right
            if m < 7:
                tile = stage[m + 1]
                left_next = pltpu.roll(tile, 96, 1)
            else:
                left_next = zeros
            emit(2 * m + 1, jnp.where(lanes < 96, left, left_next))
            left = left_next
        pltpu.make_async_copy(done.at[j], fine.at[j], out_sem.at[j]).start()
        return carry

    lax.fori_loop(0, slots, one, 0)
    for j in range(slots):
        pltpu.make_async_copy(done.at[j], fine.at[j], out_sem.at[j]).wait()

def refine(info, tags, patches, moved, planes, weights):
    return pl.pallas_call(
        refine_kernel,
        out_shape=jax.ShapeDtypeStruct((8, 64, 4096), jnp.bfloat16),
        in_specs=[pl.BlockSpec(memory_space=pltpu.SMEM)] * 2 + [pl.BlockSpec(memory_space=pl.ANY)] * 2 + [pl.BlockSpec(memory_space=pltpu.VMEM)] * 2,
        out_specs=pl.BlockSpec(memory_space=pl.ANY),
        scratch_shapes=[pltpu.VMEM((272, 1024), jnp.float32), pltpu.VMEM((8, 64, 128), jnp.float32),
                        pltpu.VMEM((8, 64, 4096), jnp.bfloat16),
                        pltpu.SemaphoreType.DMA((8,)), pltpu.SemaphoreType.DMA((8,))],
        name="refine",
    )(info, tags, patches, moved, planes, weights)


def body(patches, counts, moves, tags):
    moved, planes, info = exchange(counts, moves, patches)
    weights = jnp.asarray(refine_weights(), jnp.bfloat16)
    return refine(info, tags, patches, moved, planes, weights)


def solution(mesh):
    in_specs = (
        P(("grp", "blk"), None, None),
        P(("grp", "blk")),
        P(("grp", "blk"), None),
        P("grp", None),
    )
    out_specs = P(("grp", "blk"), None, None)
    return jax.shard_map(body, mesh=mesh, in_specs=in_specs, out_specs=out_specs, check_vma=False)
```

```python
import jax
import jax.numpy as jnp
import numpy as np
from jax import lax
from jax.experimental import pallas as pl
from jax.experimental.pallas import tpu as pltpu
from jax.sharding import PartitionSpec as P

MOST = 3
STEPS = 4
MESH = pl.DeviceIdType.MESH
SIDE = 4
CAP = 8
HELD = CAP - 1
OWN = SIDE * HELD
CROSS = MOST * STEPS
PARTS = 4
FAR = 1000

def exchange_kernel(counts, moves, patches, moved, planes, info, *scratch):
    scratch = list(scratch)
    def take(number):
        out = scratch[:number]
        del scratch[:number]
        return out
    pool, crossing_in, crossing_out, final = take(PARTS), take(PARTS), take(PARTS), take(PARTS)
    table, numbers, cuts, above, wanted, corner, edges, bases, tops = take(9)
    (pool_send, pool_recv, pool_local, cross_send, cross_recv, final_send, final_recv, final_local,
     meta_send, meta_recv, small, plane_send, plane_recv, base_send, base_recv, top_send) = scratch

    grp, blk = lax.axis_index("grp"), lax.axis_index("blk")
    groups, devices = lax.axis_size("grp"), lax.axis_size("blk")
    row, place = lax.div(blk, SIDE), lax.rem(blk, SIDE)
    rows_of_devices = devices // SIDE
    width = patches.shape[2] // PARTS
    depth = patches.shape[1] // SIDE
    line = grp * devices + blk
    after = lax.rem(line + 1, groups * devices)
    before = lax.rem(line + groups * devices - 1, groups * devices)
    after, before = [(lax.div(other, devices), lax.rem(other, devices)) for other in (after, before)]

    def across(k):
        return lax.rem(place + k, SIDE)

    def beside(k):
        return (grp, row * SIDE + across(k))

    def over(k):
        return (grp, lax.rem(row + k, rows_of_devices) * SIDE + place)

    def remote(src, dst, send, recv, device):
        return pltpu.make_async_remote_copy(src_ref=src, dst_ref=dst, send_sem=send, recv_sem=recv, device_id=device, device_id_type=MESH)

    def lanes(part):
        return pl.ds(width * part, width)

    def strip(home):
        return pl.ds(pl.multiple_of(home * depth, depth), depth)

    local = [pltpu.make_async_copy(patches.at[pl.ds(1, HELD), strip(place), lanes(i)], pool[i].at[pl.ds(HELD * place, HELD)], pool_local.at[i]) for i in range(PARTS)]
    ends = [pltpu.make_async_copy(patches.at[0, pl.ds(0, 8)], corner.at[0], small.at[0]),
            pltpu.make_async_copy(patches.at[0, pl.ds(patches.shape[1] - 8, 8)], corner.at[1], small.at[1])]
    for copy in ends + local:
        copy.start()
    lane = lax.broadcasted_iota(jnp.int32, (1, 128), 1)
    mine = jnp.where(lane == 0, counts[0], 0)
    for s in range(STEPS):
        mine = jnp.where(lane == 1 + s, moves[0, s], mine)
    table[blk] = mine

    barrier = pltpu.get_barrier_semaphore()
    for k in range(1, SIDE):
        pl.semaphore_signal(barrier, inc=1, device_id=beside(k), device_id_type=MESH)
    for k in range(1, rows_of_devices):
        pl.semaphore_signal(barrier, inc=1, device_id=over(k), device_id_type=MESH)
    first, last = place == 0, place == SIDE - 1
    @pl.when(last)
    def _():
        pl.semaphore_signal(barrier, inc=1, device_id=after, device_id_type=MESH)
    @pl.when(first)
    def _():
        pl.semaphore_signal(barrier, inc=1, device_id=before, device_id_type=MESH)
    pl.semaphore_wait(barrier, SIDE - 1 + rows_of_devices - 1 + jnp.where(first, 1, 0) + jnp.where(last, 1, 0))

    row_meta = [remote(table.at[blk], table.at[blk], meta_send.at[k - 1], meta_recv.at[k - 1], beside(k)) for k in range(1, SIDE)]
    for copy in row_meta:
        copy.start()
    gathers = [[remote(patches.at[pl.ds(1, HELD), strip(across(k)), lanes(i)], pool[i].at[pl.ds(HELD * place, HELD)],
                       pool_send.at[i, k - 1], pool_recv.at[i, k - 1], beside(k)) for k in range(1, SIDE)] for i in range(PARTS)]
    for part in gathers:
        for copy in part:
            copy.start()

    for copy in ends:
        copy.wait()
    edges[0] = corner[0, pl.ds(0, 1), :]
    edges[1] = corner[1, pl.ds(7, 1), :]

    own_row = pl.ds(row * SIDE, SIDE)
    for copy in row_meta:
        copy.wait_recv()
    read_row = pltpu.make_async_copy(table.at[own_row], numbers.at[own_row], small.at[2])
    read_row.start()
    column_meta = [remote(table.at[own_row], table.at[own_row], meta_send.at[SIDE - 2 + k], meta_recv.at[SIDE - 2 + k], over(k)) for k in range(1, rows_of_devices)]
    for copy in column_meta:
        copy.start()
    upper = remote(edges.at[0], planes.at[1], plane_send, plane_recv.at[1], before)
    upper.start()
    base = remote(edges.at[1], bases.at[place], base_send, base_recv.at[place], (grp, row * SIDE + SIDE - 1))
    base_here = pltpu.make_async_copy(edges.at[1], bases.at[SIDE - 1], base_send)
    @pl.when(jnp.logical_not(last))
    def _():
        base.start()
    @pl.when(last)
    def _():
        base_here.start()
    read_row.wait()

    def number(rank, column):
        return numbers[lax.rem(row * SIDE + rank - 1 + devices, devices), 0, column]

    def levels(known):
        live = [number(rank, 0) for rank in range(1, SIDE + 1)]
        for s in range(STEPS):
            sent = [number(rank, 1 + s) for rank in range(1, SIDE + 1)]
            came = [number(0, 1 + s) if known else 0] + sent[:-1]
            cut = [have - gone for have, gone in zip(live, sent)]
            for rank in range(1, SIDE + 1):
                cuts[8 * s + rank] = cut[rank - 1]
                above[8 * s + rank] = cut[rank - 2] if rank > 1 else OWN + MOST * s
            live = [stay + new for stay, new in zip(cut, came)]
        return live

    for s in range(STEPS):
        cuts[8 * s] = FAR
        above[8 * s] = 0
    levels(False)

    def traced(rank, slot, steps):
        for s in reversed(range(steps)):
            beyond = slot - cuts[8 * s + rank]
            came = beyond >= 0
            slot = jnp.where(came, above[8 * s + rank] + beyond, slot)
            rank = jnp.where(came, rank - 1, rank)
            rank = jnp.maximum(rank, 0)
        return jnp.where(rank == 0, slot, HELD * (rank - 1) + slot - 1)

    for s in range(STEPS):
        for t in range(MOST):
            slot = cuts[8 * s + SIDE] + t
            wanted[32 + MOST * s + t] = jnp.clip(traced(jnp.int32(SIDE), slot, s), 0, OWN - 1)

    crosses = [remote(crossing_out[i], crossing_in[i], cross_send.at[i], cross_recv.at[i], over(1)) for i in range(PARTS)]

    def cross(i):
        local[i].wait()
        for copy in gathers[i]:
            copy.wait_recv()
        for n in range(CROSS):
            crossing_out[i][n] = pool[i][wanted[32 + n]]
        crosses[i].start()

    cross(0)

    for copy in column_meta:
        copy.wait_recv()
    read = pltpu.make_async_copy(table, numbers, small.at[3])
    read.start()
    read.wait()
    live = levels(True)

    def plan(n, carry):
        rank, slot = lax.div(n, HELD) + 1, lax.rem(n, HELD) + 1
        wanted[n] = jnp.clip(traced(rank, slot, STEPS), 0, OWN + CROSS - 1)
        return carry
    lax.fori_loop(0, OWN, plan, 0)

    for i in range(1, PARTS - 1):
        cross(i)

    scatters = [[remote(final[i].at[pl.ds(HELD * across(k), HELD)], moved.at[:, strip(place), lanes(i)],
                        final_send.at[i, k - 1], final_recv.at[i, k - 1], beside(k)) for k in range(1, SIDE)] for i in range(PARTS)]
    stays = [pltpu.make_async_copy(final[i].at[pl.ds(HELD * place, HELD)], moved.at[:, strip(place), lanes(i)], final_local.at[i]) for i in range(PARTS)]
    @pl.when(last)
    def _():
        for k in range(SIDE - 1):
            remote(edges.at[1], bases.at[k], base_send, base_recv.at[k], beside(1)).wait_recv()
        base_here.wait()
    for i in range(PARTS):
        if i == 1:
            cross(PARTS - 1)
        crosses[i].wait_recv()
        def pick(n, carry, i=i):
            source = wanted[n]
            own = pool[i][jnp.minimum(source, OWN - 1)]
            other = crossing_in[i][jnp.maximum(source - OWN, 0)]
            final[i][n] = jnp.where(source < OWN, own, other)
            return carry
        lax.fori_loop(0, OWN, pick, 0, unroll=7)
        for copy in scatters[i]:
            copy.start()
        stays[i].start()
        @pl.when(last)
        def _():
            for k in range(SIDE):
                top = final[i][HELD * k + jnp.maximum(live[k] - 2, 0), pl.ds(depth - 1, 1), :]
                tops[k, :, lanes(i)] = jnp.where(live[k] > 1, top, bases[k, :, lanes(i)])
    def moved_by(rank):
        total = numbers[rank, 0, 1]
        for s in range(1, STEPS):
            total = total + numbers[rank, 0, 1 + s]
        return total

    gone_before = moved_by(lax.rem(blk + devices - 1, devices))
    info[0] = numbers[blk, 0, 0] - moved_by(blk) + gone_before
    lower_counts = jnp.int32(0)
    for rank in range(devices):
        lower_counts = lower_counts + jnp.where(rank < blk, numbers[rank, 0, 0], 0)
    info[1] = jnp.where(blk == 0, 0, lower_counts - gone_before + moved_by(devices - 1))
    info[2] = jnp.where(line > 0, 1, 0)
    info[3] = jnp.where(line < groups * devices - 1, 1, 0)

    top_copies = [remote(tops.at[k], planes.at[0], top_send.at[k], plane_recv.at[0], beside(k + 2)) for k in range(SIDE - 2)]
    top_copies.append(remote(tops.at[SIDE - 1], planes.at[0], top_send.at[SIDE - 1], plane_recv.at[0], after))
    top_here = pltpu.make_async_copy(tops.at[SIDE - 2], planes.at[0], plane_recv.at[0])
    @pl.when(last)
    def _():
        for copy in top_copies:
            copy.start()
        top_here.start()
        for copy in top_copies:
            copy.wait_send()
    @pl.when(jnp.logical_not(last))
    def _():
        base.wait_send()
    top_copies[0].wait_recv()
    upper.wait()
    for copy in row_meta + column_meta:
        copy.wait_send()
    for i in range(PARTS):
        crosses[i].wait_send()
        for copy in gathers[i]:
            copy.wait_send()
        stays[i].wait()
        for copy in scatters[i]:
            copy.wait()

def exchange(counts, moves, patches):
    slots, edge, width = patches.shape
    part = width // PARTS
    strip = edge // SIDE
    def blocks(number):
        return [pltpu.VMEM((number, strip, part), jnp.float32)] * PARTS
    dma = pltpu.SemaphoreType.DMA
    others = SIDE - 1
    return pl.pallas_call(
        exchange_kernel,
        out_shape=(jax.ShapeDtypeStruct((HELD, edge, width), jnp.float32),
                   jax.ShapeDtypeStruct((2, 1, width), jnp.float32),
                   jax.ShapeDtypeStruct((8,), jnp.int32)),
        in_specs=[pl.BlockSpec(memory_space=pltpu.SMEM)] * 2 + [pl.BlockSpec(memory_space=pl.ANY)],
        out_specs=(pl.BlockSpec(memory_space=pl.ANY), pl.BlockSpec(memory_space=pl.ANY), pl.BlockSpec(memory_space=pltpu.SMEM)),
        scratch_shapes=blocks(OWN) + blocks(CROSS) + blocks(CROSS) + blocks(OWN) + [
            pltpu.VMEM((16, 1, 128), jnp.int32), pltpu.SMEM((16, 1, 128), jnp.int32),
            pltpu.SMEM((8 * STEPS,), jnp.int32), pltpu.SMEM((8 * STEPS,), jnp.int32), pltpu.SMEM((48,), jnp.int32),
            pltpu.VMEM((2, 8, width), jnp.float32), pltpu.VMEM((2, 1, width), jnp.float32),
            pltpu.VMEM((SIDE, 1, width), jnp.float32), pltpu.VMEM((SIDE, 1, width), jnp.float32),
            dma((PARTS, others)), dma((PARTS, others)), dma((PARTS,)), dma((PARTS,)), dma((PARTS,)),
            dma((PARTS, others)), dma((PARTS, others)), dma((PARTS,)),
            dma((2 * others,)), dma((2 * others,)), dma((4,)), dma(()), dma((2,)), dma(()), dma((SIDE,)), dma((SIDE,)),
        ],
        compiler_params=pltpu.CompilerParams(collective_id=0, has_side_effects=True),
        name="exchange",
    )(counts, moves, patches)


def refine_weights():
    fine = np.arange(64)
    home, side = fine // 2, fine // 2 + 2 * (fine % 2) - 1
    grid = np.arange(32)[:, None]
    z = 0.75 * (grid == home) + 0.25 * (grid == side)
    y = np.zeros((4, 2, 2), np.float32)
    for c in range(2):
        y[c + 1, c, :] = 0.75
        y[c, c, 0] = 0.25
        y[c + 2, c, 1] = 0.25
    half = np.kron(y.reshape(4, 4), z)
    return np.concatenate([half, half], 0)

def refine_kernel(info, tags, patches, moved, planes, weights, fine, rows, stage, done, in_sem, out_sem):
    slots, edge = patches.shape[0], patches.shape[1]
    loads = [pltpu.make_async_copy(moved.at[j - 1] if j else patches.at[0], rows.at[pl.ds(8 + edge * j, edge)], in_sem.at[j]) for j in range(slots)]
    for load in loads:
        load.start()
    live, offset = info[0], info[1]
    for load in loads:
        load.wait()
    rows[pl.ds(7, 1), :] = jnp.where(info[2] == 0, 0.0, planes[0])
    rows[pl.ds(8 + edge * live, 1), :] = jnp.where(info[3] == 0, 0.0, planes[1])
    lanes = lax.broadcasted_iota(jnp.int32, (2 * edge, 128), 1)
    zeros = jnp.zeros((2 * edge, 128), jnp.float32)

    def one(j, carry):
        start = pl.multiple_of(edge * j, 8)
        tag = tags[0, jnp.minimum(offset + j, tags.shape[1] - 1)]
        factor = jnp.where(j < live, 1.0 + 0.5 * tag.astype(jnp.float32), 0.0)
        for m in range(8):
            part = rows[pl.ds(start, edge + 16), pl.ds(128 * m, 128)] * factor
            home = 0.75 * part[8:8 + edge]
            quarter = 0.25 * part
            stage[m, pl.ds(0, edge, stride=2), :] = home + quarter[7:7 + edge]
            stage[m, pl.ds(1, edge, stride=2), :] = home + quarter[9:9 + edge]
        def emit(window, value):
            high = value.astype(jnp.bfloat16)
            low = (value - high.astype(jnp.float32)).astype(jnp.bfloat16)
            both = jnp.concatenate([high, low], axis=1)
            got = jnp.dot(both, weights[...], preferred_element_type=jnp.float32)
            done[j, :, pl.ds(256 * window, 256)] = got.astype(jnp.bfloat16)
        right_before = zeros
        tile = stage[0]
        left = pltpu.roll(tile, 96, 1)
        for m in range(8):
            right = pltpu.roll(tile, 32, 1)
            emit(2 * m, jnp.where(lanes < 32, right_before, right))
            right_before = right
            if m < 7:
                tile = stage[m + 1]
                left_next = pltpu.roll(tile, 96, 1)
            else:
                left_next = zeros
            emit(2 * m + 1, jnp.where(lanes < 96, left, left_next))
            left = left_next
        pltpu.make_async_copy(done.at[j], fine.at[j], out_sem.at[j]).start()
        return carry

    lax.fori_loop(0, slots, one, 0, unroll=4)
    for j in range(slots):
        pltpu.make_async_copy(done.at[j], fine.at[j], out_sem.at[j]).wait()

def refine(info, tags, patches, moved, planes, weights):
    return pl.pallas_call(
        refine_kernel,
        out_shape=jax.ShapeDtypeStruct((8, 64, 4096), jnp.bfloat16),
        in_specs=[pl.BlockSpec(memory_space=pltpu.SMEM)] * 2 + [pl.BlockSpec(memory_space=pl.ANY)] * 2 + [pl.BlockSpec(memory_space=pltpu.VMEM)] * 2,
        out_specs=pl.BlockSpec(memory_space=pl.ANY),
        scratch_shapes=[pltpu.VMEM((272, 1024), jnp.float32), pltpu.VMEM((8, 64, 128), jnp.float32),
                        pltpu.VMEM((8, 64, 4096), jnp.bfloat16),
                        pltpu.SemaphoreType.DMA((8,)), pltpu.SemaphoreType.DMA((8,))],
        name="refine",
    )(info, tags, patches, moved, planes, weights)


def body(patches, counts, moves, tags):
    moved, planes, info = exchange(counts, moves, patches)
    weights = jnp.asarray(refine_weights(), jnp.bfloat16)
    return refine(info, tags, patches, moved, planes, weights)


def solution(mesh):
    in_specs = (
        P(("grp", "blk"), None, None),
        P(("grp", "blk")),
        P(("grp", "blk"), None),
        P("grp", None),
    )
    out_specs = P(("grp", "blk"), None, None)
    return jax.shard_map(body, mesh=mesh, in_specs=in_specs, out_specs=out_specs, check_vma=False)
```

```python
import jax
import jax.numpy as jnp
import numpy as np
from jax import lax
from jax.experimental import pallas as pl
from jax.experimental.pallas import tpu as pltpu
from jax.sharding import PartitionSpec as P

MOST = 3
STEPS = 4
MESH = pl.DeviceIdType.MESH
SIDE = 4
CAP = 8
HELD = CAP - 1
OWN = SIDE * HELD
CROSS = MOST * STEPS
PARTS = 4
FAR = 1000

def exchange_kernel(counts_in, moves_in, patches, moved, planes, info_out, *scratch):
    scratch = list(scratch)
    def take(number):
        out = scratch[:number]
        del scratch[:number]
        return out
    counts, moves, info = take(3)
    pool, crossing_in, crossing_out, final = take(PARTS), take(PARTS), take(PARTS), take(PARTS)
    table, numbers, cuts, above, wanted, corner, edges, bases, tops = take(9)
    (pool_send, pool_recv, pool_local, cross_send, cross_recv, final_send, final_recv, final_local,
     meta_send, meta_recv, small, plane_send, plane_recv, base_send, base_recv, top_send, ready) = scratch

    grp, blk = lax.axis_index("grp"), lax.axis_index("blk")
    groups, devices = lax.axis_size("grp"), lax.axis_size("blk")
    row, place = lax.div(blk, SIDE), lax.rem(blk, SIDE)
    rows_of_devices = devices // SIDE
    width = patches.shape[2] // PARTS
    depth = patches.shape[1] // SIDE
    line = grp * devices + blk
    after = lax.rem(line + 1, groups * devices)
    before = lax.rem(line + groups * devices - 1, groups * devices)
    after, before = [(lax.div(other, devices), lax.rem(other, devices)) for other in (after, before)]

    def across(k):
        return lax.rem(place + k, SIDE)

    def beside(k):
        return (grp, row * SIDE + across(k))

    def over(k):
        return (grp, lax.rem(row + k, rows_of_devices) * SIDE + place)

    def remote(src, dst, send, recv, device):
        return pltpu.make_async_remote_copy(src_ref=src, dst_ref=dst, send_sem=send, recv_sem=recv, device_id=device, device_id_type=MESH)

    def lanes(part):
        return pl.ds(width * part, width)

    def strip(home):
        return pl.ds(pl.multiple_of(home * depth, depth), depth)

    first, last = place == 0, place == SIDE - 1
    opening, closing = blk == 0, blk == devices - 1
    next_group = (lax.rem(grp + 1, groups), 0)
    last_group = (lax.rem(grp + groups - 1, groups), 0)
    barrier = pltpu.get_barrier_semaphore()
    for k in range(1, SIDE):
        pl.semaphore_signal(barrier, inc=1, device_id=beside(k), device_id_type=MESH)
    for k in range(1, rows_of_devices):
        pl.semaphore_signal(barrier, inc=1, device_id=over(k), device_id_type=MESH)
    @pl.when(last)
    def _():
        pl.semaphore_signal(barrier, inc=1, device_id=(grp, lax.rem(blk + 1, devices)), device_id_type=MESH)
    @pl.when(first)
    def _():
        pl.semaphore_signal(barrier, inc=1, device_id=(grp, lax.rem(blk + devices - 1, devices)), device_id_type=MESH)
    @pl.when(opening)
    def _():
        pl.semaphore_signal(barrier, inc=1, device_id=next_group, device_id_type=MESH)
        pl.semaphore_signal(barrier, inc=1, device_id=last_group, device_id_type=MESH)

    local = [pltpu.make_async_copy(patches.at[pl.ds(1, HELD), strip(place), lanes(i)], pool[i].at[pl.ds(HELD * place, HELD)], pool_local.at[i]) for i in range(PARTS)]
    ends = [pltpu.make_async_copy(patches.at[0, pl.ds(0, 8)], corner.at[0], small.at[0]),
            pltpu.make_async_copy(patches.at[0, pl.ds(patches.shape[1] - 8, 8)], corner.at[1], small.at[1])]
    given = [pltpu.make_async_copy(counts_in, counts, small.at[4]), pltpu.make_async_copy(moves_in, moves, small.at[5])]
    for copy in given + ends + local:
        copy.start()
    for copy in given:
        copy.wait()
    lane = lax.broadcasted_iota(jnp.int32, (1, 128), 1)
    mine = jnp.where(lane == 0, counts[0], 0)
    for s in range(STEPS):
        mine = jnp.where(lane == 1 + s, moves[0, s], mine)
    table[blk] = mine

    pl.semaphore_wait(barrier, SIDE - 1 + rows_of_devices - 1 + jnp.where(first, 1, 0) + jnp.where(last, 1, 0) + jnp.where(opening, 2, 0))
    @pl.when(opening)
    def _():
        pl.semaphore_signal(ready, inc=1, device_id=(grp, devices - 1), device_id_type=MESH)
        pl.semaphore_signal(ready, inc=1, device_id=next_group, device_id_type=MESH)

    row_meta = [remote(table.at[blk], table.at[blk], meta_send.at[k - 1], meta_recv.at[k - 1], beside(k)) for k in range(1, SIDE)]
    for copy in row_meta:
        copy.start()
    gathers = [[remote(patches.at[pl.ds(1, HELD), strip(across(k)), lanes(i)], pool[i].at[pl.ds(HELD * place, HELD)],
                       pool_send.at[i, k - 1], pool_recv.at[i, k - 1], beside(k)) for k in range(1, SIDE)] for i in range(PARTS)]
    for part in gathers:
        for copy in part:
            copy.start()

    for copy in ends:
        copy.wait()
    edges[0] = corner[0, pl.ds(0, 1), :]
    edges[1] = corner[1, pl.ds(7, 1), :]

    own_row = pl.ds(row * SIDE, SIDE)
    for copy in row_meta:
        copy.wait_recv()
    read_row = pltpu.make_async_copy(table.at[own_row], numbers.at[own_row], small.at[2])
    read_row.start()
    column_meta = [remote(table.at[own_row], table.at[own_row], meta_send.at[SIDE - 2 + k], meta_recv.at[SIDE - 2 + k], over(k)) for k in range(1, rows_of_devices)]
    for copy in column_meta:
        copy.start()
    upper = remote(edges.at[0], planes.at[1], plane_send, plane_recv.at[1], before)
    base = remote(edges.at[1], bases.at[place], base_send, base_recv.at[place], (grp, row * SIDE + SIDE - 1))
    base_here = pltpu.make_async_copy(edges.at[1], bases.at[SIDE - 1], base_send)
    @pl.when(jnp.logical_not(last))
    def _():
        base.start()
    @pl.when(last)
    def _():
        base_here.start()
    read_row.wait()

    def number(rank, column):
        return numbers[lax.rem(row * SIDE + rank - 1 + devices, devices), 0, column]

    def levels(known):
        live = [number(rank, 0) for rank in range(1, SIDE + 1)]
        for s in range(STEPS):
            sent = [number(rank, 1 + s) for rank in range(1, SIDE + 1)]
            came = [number(0, 1 + s) if known else 0] + sent[:-1]
            cut = [have - gone for have, gone in zip(live, sent)]
            for rank in range(1, SIDE + 1):
                cuts[8 * s + rank] = cut[rank - 1]
                above[8 * s + rank] = cut[rank - 2] if rank > 1 else OWN + MOST * s
            live = [stay + new for stay, new in zip(cut, came)]
        return live

    for s in range(STEPS):
        cuts[8 * s] = FAR
        above[8 * s] = 0
    levels(False)

    def traced(rank, slot, steps):
        for s in reversed(range(steps)):
            beyond = slot - cuts[8 * s + rank]
            came = beyond >= 0
            slot = jnp.where(came, above[8 * s + rank] + beyond, slot)
            rank = jnp.where(came, rank - 1, rank)
            rank = jnp.maximum(rank, 0)
        return jnp.where(rank == 0, slot, HELD * (rank - 1) + slot - 1)

    for s in range(STEPS):
        for t in range(MOST):
            slot = cuts[8 * s + SIDE] + t
            wanted[32 + MOST * s + t] = jnp.clip(traced(jnp.int32(SIDE), slot, s), 0, OWN - 1)

    crosses = [remote(crossing_out[i], crossing_in[i], cross_send.at[i], cross_recv.at[i], over(1)) for i in range(PARTS)]

    def cross(i):
        local[i].wait()
        for copy in gathers[i]:
            copy.wait_recv()
        for n in range(CROSS):
            crossing_out[i][n] = pool[i][wanted[32 + n]]
        crosses[i].start()

    cross(0)

    @pl.when(opening)
    def _():
        pl.semaphore_wait(ready, 1)
    upper.start()
    for copy in column_meta:
        copy.wait_recv()
    read = pltpu.make_async_copy(table, numbers, small.at[3])
    read.start()
    read.wait()
    live = levels(True)

    def plan(n, carry):
        rank, slot = lax.div(n, HELD) + 1, lax.rem(n, HELD) + 1
        wanted[n] = jnp.clip(traced(rank, slot, STEPS), 0, OWN + CROSS - 1)
        return carry
    lax.fori_loop(0, OWN, plan, 0)

    for i in range(1, PARTS - 1):
        cross(i)

    scatters = [[remote(final[i].at[pl.ds(HELD * across(k), HELD)], moved.at[:, strip(place), lanes(i)],
                        final_send.at[i, k - 1], final_recv.at[i, k - 1], beside(k)) for k in range(1, SIDE)] for i in range(PARTS)]
    stays = [pltpu.make_async_copy(final[i].at[pl.ds(HELD * place, HELD)], moved.at[:, strip(place), lanes(i)], final_local.at[i]) for i in range(PARTS)]
    @pl.when(last)
    def _():
        for k in range(SIDE - 1):
            remote(edges.at[1], bases.at[k], base_send, base_recv.at[k], beside(1)).wait_recv()
        base_here.wait()
    for i in range(PARTS):
        if i == 1:
            cross(PARTS - 1)
        crosses[i].wait_recv()
        def pick(n, carry, i=i):
            source = wanted[n]
            own = pool[i][jnp.minimum(source, OWN - 1)]
            other = crossing_in[i][jnp.maximum(source - OWN, 0)]
            final[i][n] = jnp.where(source < OWN, own, other)
            return carry
        lax.fori_loop(0, OWN, pick, 0, unroll=7)
        for copy in scatters[i]:
            copy.start()
        stays[i].start()
        @pl.when(last)
        def _():
            for k in range(SIDE):
                top = final[i][HELD * k + jnp.maximum(live[k] - 2, 0), pl.ds(depth - 1, 1), :]
                tops[k, :, lanes(i)] = jnp.where(live[k] > 1, top, bases[k, :, lanes(i)])
    def moved_by(rank):
        total = numbers[rank, 0, 1]
        for s in range(1, STEPS):
            total = total + numbers[rank, 0, 1 + s]
        return total

    gone_before = moved_by(lax.rem(blk + devices - 1, devices))
    info[0] = numbers[blk, 0, 0] - moved_by(blk) + gone_before
    lower_counts = jnp.int32(0)
    for rank in range(devices):
        lower_counts = lower_counts + jnp.where(rank < blk, numbers[rank, 0, 0], 0)
    info[1] = jnp.where(blk == 0, 0, lower_counts - gone_before + moved_by(devices - 1))
    info[2] = jnp.where(line > 0, 1, 0)
    info[3] = jnp.where(line < groups * devices - 1, 1, 0)
    for n in range(4, 8):
        info[n] = 0
    tell = pltpu.make_async_copy(info, info_out, small.at[6])
    tell.start()

    top_copies = [remote(tops.at[k], planes.at[0], top_send.at[k], plane_recv.at[0], beside(k + 2)) for k in range(SIDE - 2)]
    top_copies.append(remote(tops.at[SIDE - 1], planes.at[0], top_send.at[SIDE - 1], plane_recv.at[0], after))
    top_here = pltpu.make_async_copy(tops.at[SIDE - 2], planes.at[0], plane_recv.at[0])
    @pl.when(closing)
    def _():
        pl.semaphore_wait(ready, 1)
    @pl.when(last)
    def _():
        for copy in top_copies:
            copy.start()
        top_here.start()
        for copy in top_copies:
            copy.wait_send()
    @pl.when(jnp.logical_not(last))
    def _():
        base.wait_send()
    top_copies[0].wait_recv()
    upper.wait()
    tell.wait()
    for copy in row_meta + column_meta:
        copy.wait_send()
    for i in range(PARTS):
        crosses[i].wait_send()
        for copy in gathers[i]:
            copy.wait_send()
        stays[i].wait()
        for copy in scatters[i]:
            copy.wait()

def exchange(counts, moves, patches):
    slots, edge, width = patches.shape
    part = width // PARTS
    strip = edge // SIDE
    def blocks(number):
        return [pltpu.VMEM((number, strip, part), jnp.float32)] * PARTS
    dma = pltpu.SemaphoreType.DMA
    others = SIDE - 1
    return pl.pallas_call(
        exchange_kernel,
        out_shape=(jax.ShapeDtypeStruct((HELD, edge, width), jnp.float32),
                   jax.ShapeDtypeStruct((2, 1, width), jnp.float32),
                   jax.ShapeDtypeStruct((8,), jnp.int32)),
        in_specs=[pl.BlockSpec(memory_space=pl.ANY)] * 3,
        out_specs=(pl.BlockSpec(memory_space=pl.ANY),) * 3,
        scratch_shapes=[pltpu.SMEM((1,), jnp.int32), pltpu.SMEM((1, STEPS), jnp.int32), pltpu.SMEM((8,), jnp.int32)] + blocks(OWN) + blocks(CROSS) + blocks(CROSS) + blocks(OWN) + [
            pltpu.VMEM((16, 1, 128), jnp.int32), pltpu.SMEM((16, 1, 128), jnp.int32),
            pltpu.SMEM((8 * STEPS,), jnp.int32), pltpu.SMEM((8 * STEPS,), jnp.int32), pltpu.SMEM((48,), jnp.int32),
            pltpu.VMEM((2, 8, width), jnp.float32), pltpu.VMEM((2, 1, width), jnp.float32),
            pltpu.VMEM((SIDE, 1, width), jnp.float32), pltpu.VMEM((SIDE, 1, width), jnp.float32),
            dma((PARTS, others)), dma((PARTS, others)), dma((PARTS,)), dma((PARTS,)), dma((PARTS,)),
            dma((PARTS, others)), dma((PARTS, others)), dma((PARTS,)),
            dma((2 * others,)), dma((2 * others,)), dma((7,)), dma(()), dma((2,)), dma(()), dma((SIDE,)), dma((SIDE,)), pltpu.SemaphoreType.REGULAR,
        ],
        compiler_params=pltpu.CompilerParams(collective_id=0, has_side_effects=True),
        name="exchange",
    )(counts, moves, patches)


def refine_weights():
    fine = np.arange(64)
    home, side = fine // 2, fine // 2 + 2 * (fine % 2) - 1
    grid = np.arange(32)[:, None]
    z = 0.75 * (grid == home) + 0.25 * (grid == side)
    y = np.zeros((4, 2, 2), np.float32)
    for c in range(2):
        y[c + 1, c, :] = 0.75
        y[c, c, 0] = 0.25
        y[c + 2, c, 1] = 0.25
    half = np.kron(y.reshape(4, 4), z)
    return np.concatenate([half, half], 0)

def refine_kernel(info_in, tags_in, patches, moved, planes_in, weights_in, fine, info, tags, planes, weights, rows, stage, done, in_sem, small_sem, out_sem):
    slots, edge = patches.shape[0], patches.shape[1]
    loads = [pltpu.make_async_copy(moved.at[j - 1] if j else patches.at[0], rows.at[pl.ds(8 + edge * j, edge)], in_sem.at[j]) for j in range(slots)]
    small = [pltpu.make_async_copy(src, dst, small_sem.at[n]) for n, (src, dst) in enumerate([(info_in, info), (tags_in, tags), (planes_in, planes), (weights_in, weights)])]
    for load in small + loads:
        load.start()
    for load in small[:3]:
        load.wait()
    live, offset = info[0], info[1]
    rows[pl.ds(7, 1), :] = jnp.where(info[2] == 0, 0.0, planes[0])
    rows[pl.ds(8 + edge * slots, 1), :] = jnp.zeros((1, rows.shape[1]), jnp.float32)
    small[3].wait()
    group = 2
    lanes = lax.broadcasted_iota(jnp.int32, (2 * edge * group, 128), 1)
    zeros = jnp.zeros((2 * edge * group, 128), jnp.float32)

    first_row = lax.broadcasted_iota(jnp.int32, (8, 128), 0) == 0

    def some(g):
        for load in loads[0 if g == 0 else group * g + 1:group * g + group + 1]:
            load.wait()
        for half in range(group):
            j = g * group + half
            start = edge * j
            tag = tags[0, jnp.minimum(offset + j, tags.shape[1] - 1)]
            factor = jnp.where(j < live, 1.0 + 0.5 * tag.astype(jnp.float32), 0.0)
            top = j == live - 1
            for m in range(8):
                chunk = pl.ds(128 * m, 128)
                over = jnp.where(info[3] == 0, 0.0, planes[1, :, chunk])
                tail = jnp.where(jnp.logical_and(top, first_row), over, rows[pl.ds(start + edge + 8, 8), chunk])
                part = jnp.concatenate([rows[pl.ds(start, edge + 8), chunk], tail], 0) * factor
                home = 0.75 * part[8:8 + edge]
                quarter = 0.25 * part
                stage[m, pl.ds(2 * edge * half, edge, stride=2), :] = home + quarter[7:7 + edge]
                stage[m, pl.ds(2 * edge * half + 1, edge, stride=2), :] = home + quarter[9:9 + edge]
        def emit(window, value):
            high = value.astype(jnp.bfloat16)
            low = (value - high.astype(jnp.float32)).astype(jnp.bfloat16)
            both = jnp.concatenate([high, low], axis=1)
            got = jnp.dot(both, weights[...], preferred_element_type=jnp.float32)
            done[pl.ds(g * group, group), :, pl.ds(256 * window, 256)] = got.astype(jnp.bfloat16).reshape(group, 2 * edge, 256)
        right_before = zeros
        tile = stage[0]
        left = pltpu.roll(tile, 96, 1)
        for m in range(8):
            right = pltpu.roll(tile, 32, 1)
            emit(2 * m, jnp.where(lanes < 32, right_before, right))
            right_before = right
            if m < 7:
                tile = stage[m + 1]
                left_next = pltpu.roll(tile, 96, 1)
            else:
                left_next = zeros
            emit(2 * m + 1, jnp.where(lanes < 96, left, left_next))
            left = left_next
        for half in range(group):
            j = g * group + half
            pltpu.make_async_copy(done.at[j], fine.at[j], out_sem.at[j]).start()

    for g in range(slots // group):
        some(g)
    for j in range(slots):
        pltpu.make_async_copy(done.at[j], fine.at[j], out_sem.at[j]).wait()

def refine(info, tags, patches, moved, planes, weights):
    return pl.pallas_call(
        refine_kernel,
        out_shape=jax.ShapeDtypeStruct((8, 64, 4096), jnp.bfloat16),
        in_specs=[pl.BlockSpec(memory_space=pl.ANY)] * 6,
        out_specs=pl.BlockSpec(memory_space=pl.ANY),
        scratch_shapes=[pltpu.SMEM((8,), jnp.int32), pltpu.SMEM((1, 128), jnp.int32),
                        pltpu.VMEM((2, 1, 1024), jnp.float32), pltpu.VMEM((256, 256), jnp.bfloat16),
                        pltpu.VMEM((272, 1024), jnp.float32), pltpu.VMEM((8, 128, 128), jnp.float32),
                        pltpu.VMEM((8, 64, 4096), jnp.bfloat16),
                        pltpu.SemaphoreType.DMA((8,)), pltpu.SemaphoreType.DMA((4,)), pltpu.SemaphoreType.DMA((8,))],
        name="refine",
    )(info, tags, patches, moved, planes, weights)


def body(patches, counts, moves, tags):
    moved, planes, info = exchange(counts, moves, patches)
    weights = jnp.asarray(refine_weights(), jnp.bfloat16)
    return refine(info, tags, patches, moved, planes, weights)


def solution(mesh):
    in_specs = (
        P(("grp", "blk"), None, None),
        P(("grp", "blk")),
        P(("grp", "blk"), None),
        P("grp", None),
    )
    out_specs = P(("grp", "blk"), None, None)
    return jax.shard_map(body, mesh=mesh, in_specs=in_specs, out_specs=out_specs, check_vma=False)
```

```python
import jax
import jax.numpy as jnp
import numpy as np
from jax import lax
from jax.experimental import pallas as pl
from jax.experimental.pallas import tpu as pltpu
from jax.sharding import PartitionSpec as P

MOST = 3
STEPS = 4
MESH = pl.DeviceIdType.MESH
SIDE = 4
CAP = 8
HELD = CAP - 1
OWN = SIDE * HELD
CROSS = MOST * STEPS
PARTS = 4
FAR = 1000

def exchange_kernel(counts_in, moves_in, patches, moved, planes, info_out, *scratch):
    scratch = list(scratch)
    def take(number):
        out = scratch[:number]
        del scratch[:number]
        return out
    counts, moves, info = take(3)
    pool, crossing_in, crossing_out, final = take(PARTS), take(PARTS), take(PARTS), take(PARTS)
    table, numbers, cuts, above, wanted, corner, edges, bases, tops = take(9)
    (pool_send, pool_recv, pool_local, cross_send, cross_recv, final_send, final_recv, final_local,
     meta_send, meta_recv, small, plane_send, plane_recv, base_send, base_recv, top_send, ready) = scratch

    grp, blk = lax.axis_index("grp"), lax.axis_index("blk")
    groups, devices = lax.axis_size("grp"), lax.axis_size("blk")
    row, place = lax.div(blk, SIDE), lax.rem(blk, SIDE)
    rows_of_devices = devices // SIDE
    width = patches.shape[2] // PARTS
    depth = patches.shape[1] // SIDE
    line = grp * devices + blk
    after = lax.rem(line + 1, groups * devices)
    before = lax.rem(line + groups * devices - 1, groups * devices)
    after, before = [(lax.div(other, devices), lax.rem(other, devices)) for other in (after, before)]

    def across(k):
        return lax.rem(place + k, SIDE)

    def beside(k):
        return (grp, row * SIDE + across(k))

    def over(k):
        return (grp, lax.rem(row + k, rows_of_devices) * SIDE + place)

    def remote(src, dst, send, recv, device):
        return pltpu.make_async_remote_copy(src_ref=src, dst_ref=dst, send_sem=send, recv_sem=recv, device_id=device, device_id_type=MESH)

    def lanes(part):
        return pl.ds(width * part, width)

    def strip(home):
        return pl.ds(pl.multiple_of(home * depth, depth), depth)

    first, last = place == 0, place == SIDE - 1
    opening, closing = blk == 0, blk == devices - 1
    next_group = (lax.rem(grp + 1, groups), 0)
    last_group = (lax.rem(grp + groups - 1, groups), 0)
    barrier = pltpu.get_barrier_semaphore()
    for k in range(1, SIDE):
        pl.semaphore_signal(barrier, inc=1, device_id=beside(k), device_id_type=MESH)
    for k in range(1, rows_of_devices):
        pl.semaphore_signal(barrier, inc=1, device_id=over(k), device_id_type=MESH)
    @pl.when(last)
    def _():
        pl.semaphore_signal(barrier, inc=1, device_id=(grp, lax.rem(blk + 1, devices)), device_id_type=MESH)
    @pl.when(first)
    def _():
        pl.semaphore_signal(barrier, inc=1, device_id=(grp, lax.rem(blk + devices - 1, devices)), device_id_type=MESH)
    @pl.when(opening)
    def _():
        pl.semaphore_signal(barrier, inc=1, device_id=next_group, device_id_type=MESH)
        pl.semaphore_signal(barrier, inc=1, device_id=last_group, device_id_type=MESH)

    local = [pltpu.make_async_copy(patches.at[pl.ds(1, HELD), strip(place), lanes(i)], pool[i].at[pl.ds(HELD * place, HELD)], pool_local.at[i]) for i in range(PARTS)]
    ends = [pltpu.make_async_copy(patches.at[0, pl.ds(0, 8)], corner.at[0], small.at[0]),
            pltpu.make_async_copy(patches.at[0, pl.ds(patches.shape[1] - 8, 8)], corner.at[1], small.at[1])]
    given = [pltpu.make_async_copy(counts_in, counts, small.at[4]), pltpu.make_async_copy(moves_in, moves, small.at[5])]
    for copy in given + ends + local:
        copy.start()
    for copy in given:
        copy.wait()
    lane = lax.broadcasted_iota(jnp.int32, (1, 128), 1)
    mine = jnp.where(lane == 0, counts[0], 0)
    for s in range(STEPS):
        mine = jnp.where(lane == 1 + s, moves[0, s], mine)
    table[blk] = mine

    pl.semaphore_wait(barrier, SIDE - 1 + rows_of_devices - 1 + jnp.where(first, 1, 0) + jnp.where(last, 1, 0) + jnp.where(opening, 2, 0))
    @pl.when(opening)
    def _():
        pl.semaphore_signal(ready, inc=1, device_id=(grp, devices - 1), device_id_type=MESH)
        pl.semaphore_signal(ready, inc=1, device_id=next_group, device_id_type=MESH)

    row_meta = [remote(table.at[blk], table.at[blk], meta_send.at[k - 1], meta_recv.at[k - 1], beside(k)) for k in range(1, SIDE)]
    for copy in row_meta:
        copy.start()
    gathers = [[remote(patches.at[pl.ds(1, HELD), strip(across(k)), lanes(i)], pool[i].at[pl.ds(HELD * place, HELD)],
                       pool_send.at[i, k - 1], pool_recv.at[i, k - 1], beside(k)) for k in range(1, SIDE)] for i in range(PARTS)]
    for part in gathers:
        for copy in part:
            copy.start()

    for copy in ends:
        copy.wait()
    edges[0] = corner[0, pl.ds(0, 1), :]
    edges[1] = corner[1, pl.ds(7, 1), :]

    own_row = pl.ds(row * SIDE, SIDE)
    for copy in row_meta:
        copy.wait_recv()
    read_row = pltpu.make_async_copy(table.at[own_row], numbers.at[own_row], small.at[2])
    read_row.start()
    column_meta = [remote(table.at[own_row], table.at[own_row], meta_send.at[SIDE - 2 + k], meta_recv.at[SIDE - 2 + k], over(k)) for k in range(1, rows_of_devices)]
    for copy in column_meta:
        copy.start()
    upper = remote(edges.at[0], planes.at[1], plane_send, plane_recv.at[1], before)
    base = remote(edges.at[1], bases.at[place], base_send, base_recv.at[place], (grp, row * SIDE + SIDE - 1))
    base_here = pltpu.make_async_copy(edges.at[1], bases.at[SIDE - 1], base_send)
    @pl.when(jnp.logical_not(last))
    def _():
        base.start()
    @pl.when(last)
    def _():
        base_here.start()
    read_row.wait()

    def number(rank, column):
        return numbers[lax.rem(row * SIDE + rank - 1 + devices, devices), 0, column]

    def levels(known):
        live = [number(rank, 0) for rank in range(1, SIDE + 1)]
        for s in range(STEPS):
            sent = [number(rank, 1 + s) for rank in range(1, SIDE + 1)]
            came = [number(0, 1 + s) if known else 0] + sent[:-1]
            cut = [have - gone for have, gone in zip(live, sent)]
            for rank in range(1, SIDE + 1):
                cuts[8 * s + rank] = cut[rank - 1]
                above[8 * s + rank] = cut[rank - 2] if rank > 1 else OWN + MOST * s
            live = [stay + new for stay, new in zip(cut, came)]
        return live

    for s in range(STEPS):
        cuts[8 * s] = FAR
        above[8 * s] = 0
    levels(False)

    def traced(rank, slot, steps):
        for s in reversed(range(steps)):
            beyond = slot - cuts[8 * s + rank]
            came = beyond >= 0
            slot = jnp.where(came, above[8 * s + rank] + beyond, slot)
            rank = jnp.where(came, rank - 1, rank)
            rank = jnp.maximum(rank, 0)
        return jnp.where(rank == 0, slot, HELD * (rank - 1) + slot - 1)

    for s in range(STEPS):
        for t in range(MOST):
            slot = cuts[8 * s + SIDE] + t
            wanted[32 + MOST * s + t] = jnp.clip(traced(jnp.int32(SIDE), slot, s), 0, OWN - 1)

    crosses = [remote(crossing_out[i], crossing_in[i], cross_send.at[i], cross_recv.at[i], over(1)) for i in range(PARTS)]

    def cross(i):
        local[i].wait()
        for copy in gathers[i]:
            copy.wait_recv()
        for n in range(CROSS):
            crossing_out[i][n] = pool[i][wanted[32 + n]]
        crosses[i].start()

    cross(0)

    @pl.when(opening)
    def _():
        pl.semaphore_wait(ready, 1)
    upper.start()
    for copy in column_meta:
        copy.wait_recv()
    read = pltpu.make_async_copy(table, numbers, small.at[3])
    read.start()
    read.wait()
    live = levels(True)

    def plan(n, carry):
        rank, slot = lax.div(n, HELD) + 1, lax.rem(n, HELD) + 1
        wanted[n] = jnp.clip(traced(rank, slot, STEPS), 0, OWN + CROSS - 1)
        return carry
    lax.fori_loop(0, OWN, plan, 0)

    for i in range(1, PARTS - 1):
        cross(i)

    scatters = [[remote(final[i].at[pl.ds(HELD * across(k), HELD)], moved.at[:, strip(place), lanes(i)],
                        final_send.at[i, k - 1], final_recv.at[i, k - 1], beside(k)) for k in range(1, SIDE)] for i in range(PARTS)]
    stays = [pltpu.make_async_copy(final[i].at[pl.ds(HELD * place, HELD)], moved.at[:, strip(place), lanes(i)], final_local.at[i]) for i in range(PARTS)]
    @pl.when(last)
    def _():
        for k in range(SIDE - 1):
            remote(edges.at[1], bases.at[k], base_send, base_recv.at[k], beside(1)).wait_recv()
        base_here.wait()
    for i in range(PARTS):
        if i == 1:
            cross(PARTS - 1)
        crosses[i].wait_recv()
        def pick(n, carry, i=i):
            source = wanted[n]
            own = pool[i][jnp.minimum(source, OWN - 1)]
            other = crossing_in[i][jnp.maximum(source - OWN, 0)]
            final[i][n] = jnp.where(source < OWN, own, other)
            return carry
        lax.fori_loop(0, OWN, pick, 0, unroll=7)
        for copy in scatters[i]:
            copy.start()
        stays[i].start()
        @pl.when(last)
        def _():
            for k in range(SIDE):
                top = final[i][HELD * k + jnp.maximum(live[k] - 2, 0), pl.ds(depth - 1, 1), :]
                tops[k, :, lanes(i)] = jnp.where(live[k] > 1, top, bases[k, :, lanes(i)])
    def moved_by(rank):
        total = numbers[rank, 0, 1]
        for s in range(1, STEPS):
            total = total + numbers[rank, 0, 1 + s]
        return total

    gone_before = moved_by(lax.rem(blk + devices - 1, devices))
    info[0] = numbers[blk, 0, 0] - moved_by(blk) + gone_before
    lower_counts = jnp.int32(0)
    for rank in range(devices):
        lower_counts = lower_counts + jnp.where(rank < blk, numbers[rank, 0, 0], 0)
    info[1] = jnp.where(blk == 0, 0, lower_counts - gone_before + moved_by(devices - 1))
    info[2] = jnp.where(line > 0, 1, 0)
    info[3] = jnp.where(line < groups * devices - 1, 1, 0)
    for n in range(4, 8):
        info[n] = 0
    tell = pltpu.make_async_copy(info, info_out, small.at[6])
    tell.start()

    top_copies = [remote(tops.at[k], planes.at[0], top_send.at[k], plane_recv.at[0], beside(k + 2)) for k in range(SIDE - 2)]
    top_copies.append(remote(tops.at[SIDE - 1], planes.at[0], top_send.at[SIDE - 1], plane_recv.at[0], after))
    top_here = pltpu.make_async_copy(tops.at[SIDE - 2], planes.at[0], plane_recv.at[0])
    @pl.when(closing)
    def _():
        pl.semaphore_wait(ready, 1)
    @pl.when(last)
    def _():
        for copy in top_copies:
            copy.start()
        top_here.start()
        for copy in top_copies:
            copy.wait_send()
    @pl.when(jnp.logical_not(last))
    def _():
        base.wait_send()
    top_copies[0].wait_recv()
    upper.wait()
    tell.wait()
    for copy in row_meta + column_meta:
        copy.wait_send()
    for i in range(PARTS):
        crosses[i].wait_send()
        for copy in gathers[i]:
            copy.wait_send()
        stays[i].wait()
        for copy in scatters[i]:
            copy.wait()

def exchange(counts, moves, patches):
    slots, edge, width = patches.shape
    part = width // PARTS
    strip = edge // SIDE
    def blocks(number):
        return [pltpu.VMEM((number, strip, part), jnp.float32)] * PARTS
    dma = pltpu.SemaphoreType.DMA
    others = SIDE - 1
    return pl.pallas_call(
        exchange_kernel,
        out_shape=(jax.ShapeDtypeStruct((HELD, edge, width), jnp.float32),
                   jax.ShapeDtypeStruct((2, 1, width), jnp.float32),
                   jax.ShapeDtypeStruct((8,), jnp.int32)),
        in_specs=[pl.BlockSpec(memory_space=pl.ANY)] * 3,
        out_specs=(pl.BlockSpec(memory_space=pl.ANY),) * 3,
        scratch_shapes=[pltpu.SMEM((1,), jnp.int32), pltpu.SMEM((1, STEPS), jnp.int32), pltpu.SMEM((8,), jnp.int32)] + blocks(OWN) + blocks(CROSS) + blocks(CROSS) + blocks(OWN) + [
            pltpu.VMEM((16, 1, 128), jnp.int32), pltpu.SMEM((16, 1, 128), jnp.int32),
            pltpu.SMEM((8 * STEPS,), jnp.int32), pltpu.SMEM((8 * STEPS,), jnp.int32), pltpu.SMEM((48,), jnp.int32),
            pltpu.VMEM((2, 8, width), jnp.float32), pltpu.VMEM((2, 1, width), jnp.float32),
            pltpu.VMEM((SIDE, 1, width), jnp.float32), pltpu.VMEM((SIDE, 1, width), jnp.float32),
            dma((PARTS, others)), dma((PARTS, others)), dma((PARTS,)), dma((PARTS,)), dma((PARTS,)),
            dma((PARTS, others)), dma((PARTS, others)), dma((PARTS,)),
            dma((2 * others,)), dma((2 * others,)), dma((7,)), dma(()), dma((2,)), dma(()), dma((SIDE,)), dma((SIDE,)), pltpu.SemaphoreType.REGULAR,
        ],
        compiler_params=pltpu.CompilerParams(collective_id=0, has_side_effects=True),
        name="exchange",
    )(counts, moves, patches)


def refine_weights():
    fine = np.arange(64)
    home, side = fine // 2, fine // 2 + 2 * (fine % 2) - 1
    grid = np.arange(32)[:, None]
    z = 0.75 * (grid == home) + 0.25 * (grid == side)
    y = np.zeros((4, 2, 2), np.float32)
    for c in range(2):
        y[c + 1, c, :] = 0.75
        y[c, c, 0] = 0.25
        y[c + 2, c, 1] = 0.25
    half = np.kron(y.reshape(4, 4), z)
    return np.concatenate([half, half], 0)

def refine_kernel(info_in, tags_in, patches, moved, planes_in, weights_in, fine, info, tags, planes, weights, rows, stage, done, in_sem, small_sem, out_sem):
    slots, edge = patches.shape[0], patches.shape[1]
    loads = [pltpu.make_async_copy(moved.at[j - 1] if j else patches.at[0], rows.at[pl.ds(8 + edge * j, edge)], in_sem.at[j]) for j in range(slots)]
    small = [pltpu.make_async_copy(src, dst, small_sem.at[n]) for n, (src, dst) in enumerate([(info_in, info), (tags_in, tags), (planes_in, planes), (weights_in, weights)])]
    for load in small + loads:
        load.start()
    for load in small[:3]:
        load.wait()
    live, offset = info[0], info[1]
    rows[pl.ds(7, 1), :] = jnp.where(info[2] == 0, 0.0, planes[0])
    rows[pl.ds(8 + edge * slots, 1), :] = jnp.zeros((1, rows.shape[1]), jnp.float32)
    small[3].wait()
    group = 2
    lanes = lax.broadcasted_iota(jnp.int32, (2 * edge * group, 128), 1)
    zeros = jnp.zeros((2 * edge * group, 128), jnp.float32)

    first_row = lax.broadcasted_iota(jnp.int32, (8, 128), 0) == 0

    def leave(g, piece):
        part = (pl.ds(g * group, group), slice(None), pl.ds(1024 * piece, 1024))
        return pltpu.make_async_copy(done.at[part], fine.at[part], out_sem.at[g, piece])

    def some(g):
        for load in loads[0 if g == 0 else group * g + 1:group * g + group + 1]:
            load.wait()
        for half in range(group):
            j = g * group + half
            start = edge * j
            tag = tags[0, jnp.minimum(offset + j, tags.shape[1] - 1)]
            factor = jnp.where(j < live, 1.0 + 0.5 * tag.astype(jnp.float32), 0.0)
            top = j == live - 1
            for m in range(8):
                chunk = pl.ds(128 * m, 128)
                over = jnp.where(info[3] == 0, 0.0, planes[1, :, chunk])
                tail = jnp.where(jnp.logical_and(top, first_row), over, rows[pl.ds(start + edge + 8, 8), chunk])
                part = jnp.concatenate([rows[pl.ds(start, edge + 8), chunk], tail], 0) * factor
                home = 0.75 * part[8:8 + edge]
                quarter = 0.25 * part
                stage[m, pl.ds(2 * edge * half, edge, stride=2), :] = home + quarter[7:7 + edge]
                stage[m, pl.ds(2 * edge * half + 1, edge, stride=2), :] = home + quarter[9:9 + edge]
        def emit(window, value):
            high = value.astype(jnp.bfloat16)
            low = (value - high.astype(jnp.float32)).astype(jnp.bfloat16)
            both = jnp.concatenate([high, low], axis=1)
            got = jnp.dot(both, weights[...], preferred_element_type=jnp.float32)
            done[pl.ds(g * group, group), :, pl.ds(256 * window, 256)] = got.astype(jnp.bfloat16).reshape(group, 2 * edge, 256)
        right_before = zeros
        tile = stage[0]
        left = pltpu.roll(tile, 96, 1)
        for m in range(8):
            right = pltpu.roll(tile, 32, 1)
            emit(2 * m, jnp.where(lanes < 32, right_before, right))
            right_before = right
            if m < 7:
                tile = stage[m + 1]
                left_next = pltpu.roll(tile, 96, 1)
            else:
                left_next = zeros
            emit(2 * m + 1, jnp.where(lanes < 96, left, left_next))
            left = left_next
            if m % 2:
                leave(g, m // 2).start()
    for g in range(slots // group):
        some(g)
    for g in range(slots // group):
        for piece in range(4):
            leave(g, piece).wait()

def refine(info, tags, patches, moved, planes, weights):
    return pl.pallas_call(
        refine_kernel,
        out_shape=jax.ShapeDtypeStruct((8, 64, 4096), jnp.bfloat16),
        in_specs=[pl.BlockSpec(memory_space=pl.ANY)] * 6,
        out_specs=pl.BlockSpec(memory_space=pl.ANY),
        scratch_shapes=[pltpu.SMEM((8,), jnp.int32), pltpu.SMEM((1, 128), jnp.int32),
                        pltpu.VMEM((2, 1, 1024), jnp.float32), pltpu.VMEM((256, 256), jnp.bfloat16),
                        pltpu.VMEM((272, 1024), jnp.float32), pltpu.VMEM((8, 128, 128), jnp.float32),
                        pltpu.VMEM((8, 64, 4096), jnp.bfloat16),
                        pltpu.SemaphoreType.DMA((8,)), pltpu.SemaphoreType.DMA((4,)), pltpu.SemaphoreType.DMA((4, 4))],
        name="refine",
    )(info, tags, patches, moved, planes, weights)


def body(patches, counts, moves, tags):
    moved, planes, info = exchange(counts, moves, patches)
    weights = jnp.asarray(refine_weights(), jnp.bfloat16)
    return refine(info, tags, patches, moved, planes, weights)


def solution(mesh):
    in_specs = (
        P(("grp", "blk"), None, None),
        P(("grp", "blk")),
        P(("grp", "blk"), None),
        P("grp", None),
    )
    out_specs = P(("grp", "blk"), None, None)
    return jax.shard_map(body, mesh=mesh, in_specs=in_specs, out_specs=out_specs, check_vma=False)
```

```python
import jax
import jax.numpy as jnp
import numpy as np
from jax import lax
from jax.experimental import pallas as pl
from jax.experimental.pallas import tpu as pltpu
from jax.sharding import PartitionSpec as P

MOST = 3
STEPS = 4
MESH = pl.DeviceIdType.MESH
SIDE = 4
CAP = 8
HELD = CAP - 1
OWN = SIDE * HELD
CROSS = MOST * STEPS
PARTS = 4
FAR_FIRST = (1, 0, 2)
FAR = 1000

def exchange_kernel(counts_in, moves_in, patches, moved, planes, info_out, *scratch):
    scratch = list(scratch)
    def take(number):
        out = scratch[:number]
        del scratch[:number]
        return out
    counts, moves, info = take(3)
    pool, crossing_in, crossing_out, final = take(PARTS), take(PARTS), take(PARTS), take(PARTS)
    table, numbers, cuts, above, wanted, corner, edges, bases, tops = take(9)
    (pool_send, pool_recv, pool_local, cross_send, cross_recv, final_send, final_recv, final_local,
     meta_send, meta_recv, small, plane_send, plane_recv, base_send, base_recv, top_send, ready) = scratch

    grp, blk = lax.axis_index("grp"), lax.axis_index("blk")
    groups, devices = lax.axis_size("grp"), lax.axis_size("blk")
    row, place = lax.div(blk, SIDE), lax.rem(blk, SIDE)
    rows_of_devices = devices // SIDE
    width = patches.shape[2] // PARTS
    depth = patches.shape[1] // SIDE
    line = grp * devices + blk
    after = lax.rem(line + 1, groups * devices)
    before = lax.rem(line + groups * devices - 1, groups * devices)
    after, before = [(lax.div(other, devices), lax.rem(other, devices)) for other in (after, before)]

    def across(k):
        return lax.rem(place + k, SIDE)

    def beside(k):
        return (grp, row * SIDE + across(k))

    def over(k):
        return (grp, lax.rem(row + k, rows_of_devices) * SIDE + place)

    def remote(src, dst, send, recv, device):
        return pltpu.make_async_remote_copy(src_ref=src, dst_ref=dst, send_sem=send, recv_sem=recv, device_id=device, device_id_type=MESH)

    def lanes(part):
        return pl.ds(width * part, width)

    def strip(home):
        return pl.ds(pl.multiple_of(home * depth, depth), depth)

    first, last = place == 0, place == SIDE - 1
    opening, closing = blk == 0, blk == devices - 1
    next_group = (lax.rem(grp + 1, groups), 0)
    last_group = (lax.rem(grp + groups - 1, groups), 0)
    barrier = pltpu.get_barrier_semaphore()
    for k in range(1, SIDE):
        pl.semaphore_signal(barrier, inc=1, device_id=beside(k), device_id_type=MESH)
    for k in range(1, rows_of_devices):
        pl.semaphore_signal(barrier, inc=1, device_id=over(k), device_id_type=MESH)
    @pl.when(last)
    def _():
        pl.semaphore_signal(barrier, inc=1, device_id=(grp, lax.rem(blk + 1, devices)), device_id_type=MESH)
    @pl.when(first)
    def _():
        pl.semaphore_signal(barrier, inc=1, device_id=(grp, lax.rem(blk + devices - 1, devices)), device_id_type=MESH)
    @pl.when(opening)
    def _():
        pl.semaphore_signal(barrier, inc=1, device_id=next_group, device_id_type=MESH)
        pl.semaphore_signal(barrier, inc=1, device_id=last_group, device_id_type=MESH)

    local = [pltpu.make_async_copy(patches.at[pl.ds(1, HELD), strip(place), lanes(i)], pool[i].at[pl.ds(HELD * place, HELD)], pool_local.at[i]) for i in range(PARTS)]
    ends = [pltpu.make_async_copy(patches.at[0, pl.ds(0, 8)], corner.at[0], small.at[0]),
            pltpu.make_async_copy(patches.at[0, pl.ds(patches.shape[1] - 8, 8)], corner.at[1], small.at[1])]
    given = [pltpu.make_async_copy(counts_in, counts, small.at[4]), pltpu.make_async_copy(moves_in, moves, small.at[5])]
    for copy in given + ends + local:
        copy.start()
    for copy in given:
        copy.wait()
    lane = lax.broadcasted_iota(jnp.int32, (1, 128), 1)
    mine = jnp.where(lane == 0, counts[0], 0)
    for s in range(STEPS):
        mine = jnp.where(lane == 1 + s, moves[0, s], mine)
    table[blk] = mine

    pl.semaphore_wait(barrier, SIDE - 1 + rows_of_devices - 1 + jnp.where(first, 1, 0) + jnp.where(last, 1, 0) + jnp.where(opening, 2, 0))
    @pl.when(opening)
    def _():
        pl.semaphore_signal(ready, inc=1, device_id=(grp, devices - 1), device_id_type=MESH)
        pl.semaphore_signal(ready, inc=1, device_id=next_group, device_id_type=MESH)

    row_meta = [remote(table.at[blk], table.at[blk], meta_send.at[k - 1], meta_recv.at[k - 1], beside(k)) for k in range(1, SIDE)]
    for copy in row_meta:
        copy.start()
    gathers = [[remote(patches.at[pl.ds(1, HELD), strip(across(k)), lanes(i)], pool[i].at[pl.ds(HELD * place, HELD)],
                       pool_send.at[i, k - 1], pool_recv.at[i, k - 1], beside(k)) for k in range(1, SIDE)] for i in range(PARTS)]
    for part in gathers:
        for n in FAR_FIRST:
            part[n].start()

    for copy in ends:
        copy.wait()
    edges[0] = corner[0, pl.ds(0, 1), :]
    edges[1] = corner[1, pl.ds(7, 1), :]

    own_row = pl.ds(row * SIDE, SIDE)
    for copy in row_meta:
        copy.wait_recv()
    read_row = pltpu.make_async_copy(table.at[own_row], numbers.at[own_row], small.at[2])
    read_row.start()
    column_meta = [remote(table.at[own_row], table.at[own_row], meta_send.at[SIDE - 2 + k], meta_recv.at[SIDE - 2 + k], over(k)) for k in range(1, rows_of_devices)]
    for copy in column_meta:
        copy.start()
    upper = remote(edges.at[0], planes.at[1], plane_send, plane_recv.at[1], before)
    base = remote(edges.at[1], bases.at[place], base_send, base_recv.at[place], (grp, row * SIDE + SIDE - 1))
    base_here = pltpu.make_async_copy(edges.at[1], bases.at[SIDE - 1], base_send)
    @pl.when(jnp.logical_not(last))
    def _():
        base.start()
    @pl.when(last)
    def _():
        base_here.start()
    read_row.wait()

    def number(rank, column):
        return numbers[lax.rem(row * SIDE + rank - 1 + devices, devices), 0, column]

    def levels(known):
        live = [number(rank, 0) for rank in range(1, SIDE + 1)]
        for s in range(STEPS):
            sent = [number(rank, 1 + s) for rank in range(1, SIDE + 1)]
            came = [number(0, 1 + s) if known else 0] + sent[:-1]
            cut = [have - gone for have, gone in zip(live, sent)]
            for rank in range(1, SIDE + 1):
                cuts[8 * s + rank] = cut[rank - 1]
                above[8 * s + rank] = cut[rank - 2] if rank > 1 else OWN + MOST * s
            live = [stay + new for stay, new in zip(cut, came)]
        return live

    for s in range(STEPS):
        cuts[8 * s] = FAR
        above[8 * s] = 0
    levels(False)

    def traced(rank, slot, steps):
        for s in reversed(range(steps)):
            beyond = slot - cuts[8 * s + rank]
            came = beyond >= 0
            slot = jnp.where(came, above[8 * s + rank] + beyond, slot)
            rank = jnp.where(came, rank - 1, rank)
            rank = jnp.maximum(rank, 0)
        return jnp.where(rank == 0, slot, HELD * (rank - 1) + slot - 1)

    for s in range(STEPS):
        for t in range(MOST):
            slot = cuts[8 * s + SIDE] + t
            wanted[32 + MOST * s + t] = jnp.clip(traced(jnp.int32(SIDE), slot, s), 0, OWN - 1)

    crosses = [remote(crossing_out[i], crossing_in[i], cross_send.at[i], cross_recv.at[i], over(1)) for i in range(PARTS)]

    def cross(i):
        local[i].wait()
        for copy in gathers[i]:
            copy.wait_recv()
        for n in range(CROSS):
            crossing_out[i][n] = pool[i][wanted[32 + n]]
        crosses[i].start()

    cross(0)

    @pl.when(opening)
    def _():
        pl.semaphore_wait(ready, 1)
    upper.start()
    for copy in column_meta:
        copy.wait_recv()
    read = pltpu.make_async_copy(table, numbers, small.at[3])
    read.start()
    read.wait()
    live = levels(True)

    def plan(n, carry):
        rank, slot = lax.div(n, HELD) + 1, lax.rem(n, HELD) + 1
        wanted[n] = jnp.clip(traced(rank, slot, STEPS), 0, OWN + CROSS - 1)
        return carry
    lax.fori_loop(0, OWN, plan, 0)

    for i in range(1, PARTS - 1):
        cross(i)

    scatters = [[remote(final[i].at[pl.ds(HELD * across(k), HELD)], moved.at[:, strip(place), lanes(i)],
                        final_send.at[i, k - 1], final_recv.at[i, k - 1], beside(k)) for k in range(1, SIDE)] for i in range(PARTS)]
    stays = [pltpu.make_async_copy(final[i].at[pl.ds(HELD * place, HELD)], moved.at[:, strip(place), lanes(i)], final_local.at[i]) for i in range(PARTS)]
    @pl.when(last)
    def _():
        for k in range(SIDE - 1):
            remote(edges.at[1], bases.at[k], base_send, base_recv.at[k], beside(1)).wait_recv()
        base_here.wait()
    for i in range(PARTS):
        if i == 1:
            cross(PARTS - 1)
        crosses[i].wait_recv()
        def pick(n, carry, i=i):
            source = wanted[n]
            own = pool[i][jnp.minimum(source, OWN - 1)]
            other = crossing_in[i][jnp.maximum(source - OWN, 0)]
            final[i][n] = jnp.where(source < OWN, own, other)
            return carry
        lax.fori_loop(0, OWN, pick, 0, unroll=7)
        for n in FAR_FIRST:
            scatters[i][n].start()
        stays[i].start()
        @pl.when(last)
        def _():
            for k in range(SIDE):
                top = final[i][HELD * k + jnp.maximum(live[k] - 2, 0), pl.ds(depth - 1, 1), :]
                tops[k, :, lanes(i)] = jnp.where(live[k] > 1, top, bases[k, :, lanes(i)])
    def moved_by(rank):
        total = numbers[rank, 0, 1]
        for s in range(1, STEPS):
            total = total + numbers[rank, 0, 1 + s]
        return total

    gone_before = moved_by(lax.rem(blk + devices - 1, devices))
    info[0] = numbers[blk, 0, 0] - moved_by(blk) + gone_before
    lower_counts = jnp.int32(0)
    for rank in range(devices):
        lower_counts = lower_counts + jnp.where(rank < blk, numbers[rank, 0, 0], 0)
    info[1] = jnp.where(blk == 0, 0, lower_counts - gone_before + moved_by(devices - 1))
    info[2] = jnp.where(line > 0, 1, 0)
    info[3] = jnp.where(line < groups * devices - 1, 1, 0)
    for n in range(4, 8):
        info[n] = 0
    tell = pltpu.make_async_copy(info, info_out, small.at[6])
    tell.start()

    top_copies = [remote(tops.at[k], planes.at[0], top_send.at[k], plane_recv.at[0], beside(k + 2)) for k in range(SIDE - 2)]
    top_copies.append(remote(tops.at[SIDE - 1], planes.at[0], top_send.at[SIDE - 1], plane_recv.at[0], after))
    top_here = pltpu.make_async_copy(tops.at[SIDE - 2], planes.at[0], plane_recv.at[0])
    @pl.when(closing)
    def _():
        pl.semaphore_wait(ready, 1)
    @pl.when(last)
    def _():
        for copy in top_copies:
            copy.start()
        top_here.start()
        for copy in top_copies:
            copy.wait_send()
    @pl.when(jnp.logical_not(last))
    def _():
        base.wait_send()
    top_copies[0].wait_recv()
    upper.wait()
    tell.wait()
    for copy in row_meta + column_meta:
        copy.wait_send()
    for i in range(PARTS):
        crosses[i].wait_send()
        for copy in gathers[i]:
            copy.wait_send()
        stays[i].wait()
        for copy in scatters[i]:
            copy.wait()

def exchange(counts, moves, patches):
    slots, edge, width = patches.shape
    part = width // PARTS
    strip = edge // SIDE
    def blocks(number):
        return [pltpu.VMEM((number, strip, part), jnp.float32)] * PARTS
    dma = pltpu.SemaphoreType.DMA
    others = SIDE - 1
    return pl.pallas_call(
        exchange_kernel,
        out_shape=(jax.ShapeDtypeStruct((HELD, edge, width), jnp.float32),
                   jax.ShapeDtypeStruct((2, 1, width), jnp.float32),
                   jax.ShapeDtypeStruct((8,), jnp.int32)),
        in_specs=[pl.BlockSpec(memory_space=pl.ANY)] * 3,
        out_specs=(pl.BlockSpec(memory_space=pl.ANY),) * 3,
        scratch_shapes=[pltpu.SMEM((1,), jnp.int32), pltpu.SMEM((1, STEPS), jnp.int32), pltpu.SMEM((8,), jnp.int32)] + blocks(OWN) + blocks(CROSS) + blocks(CROSS) + blocks(OWN) + [
            pltpu.VMEM((16, 1, 128), jnp.int32), pltpu.SMEM((16, 1, 128), jnp.int32),
            pltpu.SMEM((8 * STEPS,), jnp.int32), pltpu.SMEM((8 * STEPS,), jnp.int32), pltpu.SMEM((48,), jnp.int32),
            pltpu.VMEM((2, 8, width), jnp.float32), pltpu.VMEM((2, 1, width), jnp.float32),
            pltpu.VMEM((SIDE, 1, width), jnp.float32), pltpu.VMEM((SIDE, 1, width), jnp.float32),
            dma((PARTS, others)), dma((PARTS, others)), dma((PARTS,)), dma((PARTS,)), dma((PARTS,)),
            dma((PARTS, others)), dma((PARTS, others)), dma((PARTS,)),
            dma((2 * others,)), dma((2 * others,)), dma((7,)), dma(()), dma((2,)), dma(()), dma((SIDE,)), dma((SIDE,)), pltpu.SemaphoreType.REGULAR,
        ],
        compiler_params=pltpu.CompilerParams(collective_id=0, has_side_effects=True),
        name="exchange",
    )(counts, moves, patches)


def refine_weights():
    fine = np.arange(64)
    home, side = fine // 2, fine // 2 + 2 * (fine % 2) - 1
    grid = np.arange(32)[:, None]
    z = 0.75 * (grid == home) + 0.25 * (grid == side)
    y = np.zeros((4, 2, 2), np.float32)
    for c in range(2):
        y[c + 1, c, :] = 0.75
        y[c, c, 0] = 0.25
        y[c + 2, c, 1] = 0.25
    half = np.kron(y.reshape(4, 4), z)
    return np.concatenate([half, half], 0)

def refine_kernel(info_in, tags_in, patches, moved, planes_in, weights_in, fine, info, tags, planes, weights, rows, stage, done, in_sem, small_sem, out_sem):
    slots, edge = patches.shape[0], patches.shape[1]
    loads = [pltpu.make_async_copy(moved.at[j - 1] if j else patches.at[0], rows.at[pl.ds(8 + edge * j, edge)], in_sem.at[j]) for j in range(slots)]
    small = [pltpu.make_async_copy(src, dst, small_sem.at[n]) for n, (src, dst) in enumerate([(info_in, info), (tags_in, tags), (planes_in, planes), (weights_in, weights)])]
    for load in small + loads:
        load.start()
    for load in small[:3]:
        load.wait()
    live, offset = info[0], info[1]
    rows[pl.ds(7, 1), :] = jnp.where(info[2] == 0, 0.0, planes[0])
    rows[pl.ds(8 + edge * slots, 1), :] = jnp.zeros((1, rows.shape[1]), jnp.float32)
    small[3].wait()
    group = 2
    lanes = lax.broadcasted_iota(jnp.int32, (2 * edge * group, 128), 1)
    zeros = jnp.zeros((2 * edge * group, 128), jnp.float32)

    first_row = lax.broadcasted_iota(jnp.int32, (8, 128), 0) == 0

    def leave(g, piece):
        part = (pl.ds(g * group, group), slice(None), pl.ds(1024 * piece, 1024))
        return pltpu.make_async_copy(done.at[part], fine.at[part], out_sem.at[g, piece])

    def some(g):
        for load in loads[0 if g == 0 else group * g + 1:group * g + group + 1]:
            load.wait()
        for half in range(group):
            j = g * group + half
            start = edge * j
            tag = tags[0, jnp.minimum(offset + j, tags.shape[1] - 1)]
            factor = jnp.where(j < live, 1.0 + 0.5 * tag.astype(jnp.float32), 0.0)
            top = j == live - 1
            for m in range(8):
                chunk = pl.ds(128 * m, 128)
                over = jnp.where(info[3] == 0, 0.0, planes[1, :, chunk])
                tail = jnp.where(jnp.logical_and(top, first_row), over, rows[pl.ds(start + edge + 8, 8), chunk])
                part = jnp.concatenate([rows[pl.ds(start, edge + 8), chunk], tail], 0) * factor
                home = 0.75 * part[8:8 + edge]
                quarter = 0.25 * part
                stage[g % 2, m, pl.ds(2 * edge * half, edge, stride=2), :] = home + quarter[7:7 + edge]
                stage[g % 2, m, pl.ds(2 * edge * half + 1, edge, stride=2), :] = home + quarter[9:9 + edge]
        def emit(window, value):
            high = value.astype(jnp.bfloat16)
            low = (value - high.astype(jnp.float32)).astype(jnp.bfloat16)
            both = jnp.concatenate([high, low], axis=1)
            got = jnp.dot(both, weights[...], preferred_element_type=jnp.float32)
            done[pl.ds(g * group, group), :, pl.ds(256 * window, 256)] = got.astype(jnp.bfloat16).reshape(group, 2 * edge, 256)
        right_before = zeros
        tile = stage[g % 2, 0]
        left = pltpu.roll(tile, 96, 1)
        for m in range(8):
            right = pltpu.roll(tile, 32, 1)
            emit(2 * m, jnp.where(lanes < 32, right_before, right))
            right_before = right
            if m < 7:
                tile = stage[g % 2, m + 1]
                left_next = pltpu.roll(tile, 96, 1)
            else:
                left_next = zeros
            emit(2 * m + 1, jnp.where(lanes < 96, left, left_next))
            left = left_next
            if m % 2:
                leave(g, m // 2).start()
    for g in range(slots // group):
        some(g)
    for g in range(slots // group):
        for piece in range(4):
            leave(g, piece).wait()

def refine(info, tags, patches, moved, planes, weights):
    return pl.pallas_call(
        refine_kernel,
        out_shape=jax.ShapeDtypeStruct((8, 64, 4096), jnp.bfloat16),
        in_specs=[pl.BlockSpec(memory_space=pl.ANY)] * 6,
        out_specs=pl.BlockSpec(memory_space=pl.ANY),
        scratch_shapes=[pltpu.SMEM((8,), jnp.int32), pltpu.SMEM((1, 128), jnp.int32),
                        pltpu.VMEM((2, 1, 1024), jnp.float32), pltpu.VMEM((256, 256), jnp.bfloat16),
                        pltpu.VMEM((272, 1024), jnp.float32), pltpu.VMEM((2, 8, 128, 128), jnp.float32),
                        pltpu.VMEM((8, 64, 4096), jnp.bfloat16),
                        pltpu.SemaphoreType.DMA((8,)), pltpu.SemaphoreType.DMA((4,)), pltpu.SemaphoreType.DMA((4, 4))],
        name="refine",
    )(info, tags, patches, moved, planes, weights)


def body(patches, counts, moves, tags):
    moved, planes, info = exchange(counts, moves, patches)
    weights = jnp.asarray(refine_weights(), jnp.bfloat16)
    return refine(info, tags, patches, moved, planes, weights)


def solution(mesh):
    in_specs = (
        P(("grp", "blk"), None, None),
        P(("grp", "blk")),
        P(("grp", "blk"), None),
        P("grp", None),
    )
    out_specs = P(("grp", "blk"), None, None)
    return jax.shard_map(body, mesh=mesh, in_specs=in_specs, out_specs=out_specs, check_vma=False)
```
